256 devices in a mesh: pipe: 8 (over x, core), ctx: 16 (over z_hi, y), tp: 2 (over z_lo).
Axes of the slice: x: 4, y: 4, z: 8 (z_hi: 4, z_lo: 2; z = z_hi * 2 + z_lo), core: 2. Of those that a mesh axis runs over, the one named last changes fastest.
Arguments:
- qkv_proj: bfloat16 [8, 3, 2048, 8192], P('pipe', None, 'ctx', 'tp'), may hold values from -6 to 6
- cotangent: bfloat16 [8, 2048, 8192], P('pipe', 'ctx', 'tp'), may hold values from -6 to 6
- block_dest: int32 [8, 256], replicated, may hold values from 0 to 255, as said below
- doc_start: int32 [8, 2048], P('pipe', 'ctx'), may hold values 0 or 1
- mr_filter: bfloat16 [8, 512, 128], P('pipe', 'tp'), may hold values from -0.5 to 0.5
Outputs:
- input_grads: bfloat16 [8, 3, 2048, 8192], P('pipe', None, ('ctx', 'tp'))
The draws below stay inside these ranges and needn't reach their ends.
Inputs may be any that keep to these rules, and one draw needn't show every extreme that they name: For each section p, block_dest[p] is a permutation of 0 .. 255. Entry d * 16 + b belongs to block b of ctx index d, and its value lies in b * 16 .. b * 16 + 15: every ctx index sends its block b to the part of the sequence held by ctx index b.
All inputs are finite; a program needn't handle non-finite values. No bound on the sum of `doc_start` on one device may be relied on, other than what follows from the above.
Results may differ from the reference program's by a relative error of at most 0.0049.
Values may be sent and summed in bfloat16 or wider, within the bound.
A program may use at most 128 MiB of HBM per device.

```python
import jax
import jax.numpy as jnp
from jax import lax

D = 8192
GROUPS = 512
MR_TAPS = 128
ROWS_DEV = 128
SECTIONS = 8
SEQ = 2048
BLOCKS_DEV = 16
NBLK = 256


def permute_slots(sub_key):
    return jax.random.permutation(sub_key, BLOCKS_DEV).astype(jnp.int32)


def draw_block_dest(key, part):
    key_list = jax.random.split(key, SECTIONS * BLOCKS_DEV)
    slot_sets = jax.vmap(permute_slots)(key_list).reshape(SECTIONS, BLOCKS_DEV, BLOCKS_DEV)
    targets = jnp.arange(BLOCKS_DEV, dtype=jnp.int32)
    result = targets[None, None, :] * BLOCKS_DEV + jnp.transpose(slot_sets, (0, 2, 1))
    return result.reshape(SECTIONS, NBLK).astype(jnp.int32)


def plant(values, key, least, high):
    extent = values.shape
    place = [jax.random.randint(jax.random.fold_in(key, axis), (), 0, extent[axis]) for axis in range(len(extent))]
    values = values.at[tuple(place)].set(least)
    longest = extent.index(max(extent))
    place[longest] = (place[longest] + 1) % extent[longest]
    return values.at[tuple(place)].set(high)


def steps_of(key, shape, cuts, least, high):
    level = 1.0
    for dim, shards_of in cuts:
        heights = jax.random.uniform(jax.random.fold_in(jax.random.fold_in(key, 6), dim), (shards_of,), jnp.float32, least / len(cuts), high / len(cuts))
        level = level * jnp.repeat(jnp.exp(heights), shape[dim] // shards_of).reshape((-1,) + (1,) * (len(shape) - 1 - dim))
    return level


def scatter_about(rng, dims, width, bound, shards=(), kind=jnp.bfloat16):
    array = jax.random.normal(rng, dims, jnp.float32) * width
    if len(shards) > 0:
        array = steps_of(rng, dims, shards, -0.22, 0.18) * array
    return jnp.clip(array, min=-bound, max=bound).astype(kind)


def setup_inputs(seed: int = 0) -> dict:
    seeds = jax.random.split(jax.random.key(seed), 6)
    qkv_proj = scatter_about(seeds[0], (SECTIONS, 3, SEQ, D), 1.0, 6.0, ((0, 8), (2, 16), (3, 2)))
    cotangent = scatter_about(seeds[1], (SECTIONS, SEQ, D), 1.0, 6.0, ((0, 8), (1, 16), (2, 2)))
    block_dest = draw_block_dest(jax.random.fold_in(seeds[5], 71), 0)
    doc_start = plant((jax.random.randint(seeds[3], (SECTIONS, SEQ), 0, 200) < 1).astype(jnp.int32), jax.random.fold_in(seeds[3], 1), 0, 1)
    mr_filter = scatter_about(seeds[4], (SECTIONS, GROUPS, MR_TAPS), MR_TAPS ** -0.5, 0.5, ((0, 8), (1, 2)))
    return dict(qkv_proj=qkv_proj, cotangent=cotangent, block_dest=block_dest, doc_start=doc_start, mr_filter=mr_filter)


def medium_conv(source, segment, filt_wide, forward):
    rim_rows = MR_TAPS - 1
    span_rows = ROWS_DEV + rim_rows
    group_size = D // GROUPS
    if forward:
        padded = jnp.concatenate([jnp.zeros((rim_rows, D), source.dtype), source], axis=0)
        seg_pad = jnp.concatenate([jnp.full((rim_rows,), -1, jnp.int32), segment])
        lag_table = jnp.arange(ROWS_DEV, dtype=jnp.int32)[:, None] + rim_rows - jnp.arange(span_rows, dtype=jnp.int32)[None, :]
    else:
        padded = jnp.concatenate([source, jnp.zeros((rim_rows, D), source.dtype)], axis=0)
        seg_pad = jnp.concatenate([segment, jnp.full((rim_rows,), -1, jnp.int32)])
        lag_table = jnp.arange(span_rows, dtype=jnp.int32)[None, :] - jnp.arange(ROWS_DEV, dtype=jnp.int32)[:, None]

    def one_block(first_row):
        window = lax.dynamic_slice_in_dim(padded, first_row, span_rows, 0).astype(jnp.float32)
        window = window.reshape(span_rows, GROUPS, group_size)
        seg_window = lax.dynamic_slice_in_dim(seg_pad, first_row, span_rows, 0)
        seg_target = lax.dynamic_slice_in_dim(segment, first_row, ROWS_DEV, 0)
        valid = (lag_table >= 0) & (lag_table < MR_TAPS) & (seg_window[None, :] == seg_target[:, None])
        picked = jnp.take(filt_wide, jnp.clip(lag_table, 0, MR_TAPS - 1), axis=1)
        toeplitz = jnp.where(valid[None], picked, jnp.float32(0.0))
        return jnp.einsum("gts,sgc->tgc", toeplitz, window, precision=lax.Precision.HIGHEST)

    block_starts = jnp.arange(SEQ // ROWS_DEV, dtype=jnp.int32) * ROWS_DEV
    return lax.map(one_block, block_starts).reshape(SEQ, D)


def one_section(qkv, grad_arrival, dest, marks_arrival, filt):
    count = dest.shape[0]
    block_rows = SEQ // count
    inverse = jnp.zeros((count,), jnp.int32).at[dest].set(jnp.arange(count, dtype=jnp.int32))

    def sequence_order(matrix):
        return jnp.take(matrix.reshape(count, block_rows, -1), inverse, axis=0).reshape(SEQ, -1)

    def arrival_order(matrix):
        return jnp.take(matrix.reshape(count, block_rows, -1), dest, axis=0).reshape(SEQ, -1)

    query = sequence_order(qkv[0])
    key_rows = sequence_order(qkv[1])
    value = sequence_order(qkv[2])
    grad_in = sequence_order(grad_arrival)
    marks = sequence_order(marks_arrival[:, None])[:, 0]
    segment = jnp.cumsum(marks, dtype=jnp.int32)
    mixed = (key_rows.astype(jnp.float32) * value.astype(jnp.float32)).astype(jnp.bfloat16)
    filt_wide = filt.astype(jnp.float32)
    medium = medium_conv(mixed, segment, filt_wide, True)
    gate_grad = (grad_in.astype(jnp.float32) * query.astype(jnp.float32)).astype(jnp.bfloat16)
    mixed_grad = medium_conv(gate_grad, segment, filt_wide, False)
    d_query = (grad_in.astype(jnp.float32) * medium).astype(jnp.bfloat16)
    d_key = (mixed_grad * value.astype(jnp.float32)).astype(jnp.bfloat16)
    d_value = (mixed_grad * key_rows.astype(jnp.float32)).astype(jnp.bfloat16)
    return jnp.stack([arrival_order(d_query), arrival_order(d_key), arrival_order(d_value)])


def reference(qkv_proj, cotangent, block_dest, doc_start, mr_filter):
    results = []
    for section in range(SECTIONS):
        results.append(one_section(qkv_proj[section], cotangent[section], block_dest[section], doc_start[section], mr_filter[section]))
    return jnp.stack([results[(section + 1) % SECTIONS] for section in range(SECTIONS)])
```

```python
import functools

import jax
import jax.numpy as jnp
from jax import lax
from jax.experimental import pallas as pl
from jax.experimental.pallas import tpu as pltpu
from jax.sharding import PartitionSpec as P

MESH = pl.DeviceIdType.MESH
F32 = jnp.float32
BF16 = jnp.bfloat16
LANES = 128
STAGES = 4


def iota(shape, dim):
    return lax.broadcasted_iota(jnp.int32, shape, dim)


def dot(a, b):
    return jnp.dot(a, b, preferred_element_type=F32)


def await_bytes(ref, sem):
    pltpu.make_async_copy(ref, ref, sem).wait()


def kernel(
    sizes,
    qkv_ref,
    cot_ref,
    dest_ref,
    marks_ref,
    filt_ref,
    out_ref,
    raw,
    stage,
    got,
    marks_all,
    taps,
    bands,
    pos_all,
    counts,
    masks,
    to_seq,
    to_arrival,
    source,
    outgoing,
    final,
    factors,
    load_sem,
    stage_send,
    stage_recv,
    mark_send,
    mark_recv,
    factor_send,
    factor_recv,
    final_send,
    final_recv,
):
    pipes, ctxs, tps = sizes
    p, c, t = lax.axis_index("pipe"), lax.axis_index("ctx"), lax.axis_index("tp")
    behind = lax.rem(p + pipes - 1, pipes)
    ahead = lax.rem(p + 1, pipes)
    rows = raw.shape[1]
    half_rows = rows // tps
    groups = taps.shape[1]
    stage_groups = groups // 2
    group_size = LANES // stage_groups

    barrier = pltpu.get_barrier_semaphore()
    for j in range(1, ctxs):
        peer = (p, lax.rem(c + j, ctxs), t)
        pl.semaphore_signal(barrier, inc=1, device_id=peer, device_id_type=MESH)
    for j in range(ctxs):
        for k in range(tps):
            peer = (ahead, lax.rem(c + j, ctxs), k)
            pl.semaphore_signal(barrier, inc=1, device_id=peer, device_id_type=MESH)

    loads = []
    for i, ref in enumerate((cot_ref.at[0], qkv_ref.at[0, 0], qkv_ref.at[0, 1], qkv_ref.at[0, 2])):
        load = pltpu.make_async_copy(ref, raw.at[i], load_sem.at[i])
        load.start()
        loads.append(load)

    def products(s):
        first, second, half = 2 * (s // 2), 2 * (s // 2) + 1, s % 2

        def one(j, carry):
            col = pl.multiple_of(j * (2 * LANES) + half * LANES, LANES)
            a = raw[first, :, pl.ds(col, LANES)].astype(F32)
            b = raw[second, :, pl.ds(col, LANES)].astype(F32)
            stage[s, j] = (a * b).reshape(rows // 8, 8, LANES).astype(BF16)
            return carry

        lax.fori_loop(0, ctxs, one, 0)

    def stage_copy(s, j):
        target = lax.rem(c + j, ctxs)
        return pltpu.make_async_remote_copy(
            src_ref=stage.at[s, target],
            dst_ref=got.at[s, c],
            send_sem=stage_send.at[s],
            recv_sem=stage_recv.at[s],
            device_id=(p, target, t),
            device_id_type=MESH,
        )

    def send_stage(s):
        for j in range(1, ctxs):
            stage_copy(s, j).start()
        got[s, c] = stage[s, c]

    loads[0].wait()
    loads[1].wait()
    products(0)
    pl.semaphore_wait(barrier, ctxs - 1 + ctxs * tps)
    for j in range(1, ctxs):
        pltpu.make_async_remote_copy(
            src_ref=marks_ref,
            dst_ref=marks_all.at[pl.ds(c, 1)],
            send_sem=mark_send,
            recv_sem=mark_recv,
            device_id=(p, lax.rem(c + j, ctxs), t),
            device_id_type=MESH,
        ).start()
    marks_all[pl.ds(c, 1)] = marks_ref[...]
    send_stage(0)
    products(1)
    send_stage(1)
    loads[2].wait()
    loads[3].wait()
    products(2)
    send_stage(2)
    products(3)
    send_stage(3)

    def factor_copies():
        copies = []
        for k in range(tps):
            span = pl.ds(k * half_rows, half_rows)
            for i, ref in enumerate((cot_ref.at[0], qkv_ref.at[0, 1], qkv_ref.at[0, 2])):
                copies.append(
                    pltpu.make_async_remote_copy(
                        src_ref=ref.at[span],
                        dst_ref=factors.at[t, i],
                        send_sem=factor_send,
                        recv_sem=factor_recv,
                        device_id=(behind, c, k),
                        device_id_type=MESH,
                    )
                )
        return copies

    mine = filt_ref[0, pl.ds(pl.multiple_of(c * groups, groups), groups), :]
    lag, lane = iota((LANES, 2 * LANES), 0), iota((LANES, 2 * LANES), 1)
    taps[0] = dot(mine, (lane == LANES - lag).astype(BF16))
    taps[1] = dot(mine, (lane == lag).astype(BF16))

    def one_band(i, carry):
        for way in range(2):
            row = jnp.broadcast_to(taps[way, pl.ds(i, 1), :], (LANES, 2 * LANES))
            band = pltpu.roll(row, 0, 1, stride=1, stride_axis=0)
            bands[way, i] = band.astype(BF16)
        return carry

    lax.fori_loop(0, groups, one_band, 0)

    slots = ctxs * ctxs
    dest = jnp.broadcast_to(dest_ref[pl.ds(p, 1), :], (ctxs, slots))
    entry, tile = iota((ctxs, slots), 1), iota((ctxs, slots), 0)
    slot = jnp.where(entry % ctxs == tile, dest - tile * ctxs, 0).astype(F32).astype(BF16)
    spread = (iota((slots, LANES), 0) // ctxs == iota((slots, LANES), 1) // 8).astype(BF16)
    pos_all[...] = dot(slot, spread) * 8.0 + (iota((ctxs, LANES), 1) % 8).astype(F32)

    await_bytes(marks_all.at[pl.ds(0, ctxs - 1)], mark_recv)
    down = iota((LANES, LANES), 0)
    across = iota((LANES, LANES), 1)
    owner = iota((ctxs, LANES), 0) == iota((ctxs, LANES), 1) // 8

    def one_order(b, table):
        pick = (down == b * 8 + across % 8).astype(BF16)
        marks = dot(marks_all[...].astype(F32).astype(BF16), pick)
        marks = jnp.sum(jnp.where(owner, marks, 0.0), axis=0, keepdims=True)
        pos = pos_all[pl.ds(b, 1), :]
        rank = down.astype(F32)
        place = (pos == rank).astype(F32)
        to_seq[b] = place.astype(BF16)
        to_arrival[b] = place.T.astype(BF16)
        count = jnp.sum(jnp.where(pos <= rank, marks, 0.0), axis=1, keepdims=True)
        return jnp.where(across == b, count, table)

    table = lax.fori_loop(0, ctxs, one_order, jnp.zeros((LANES, LANES), F32))
    counts[...] = table.T

    def one_mask(b, carry):
        here = counts[pl.ds(b, 1), :]
        total = here[:, LANES - 1 :]
        prior = counts[pl.ds(jnp.maximum(b - 1, 0), 1), :]
        prior = jnp.where(b > 0, prior - prior[:, LANES - 1 :], -1.0)
        later = counts[pl.ds(jnp.minimum(b + 1, ctxs - 1), 1), :]
        later = jnp.where(b < ctxs - 1, later + total, -1.0)
        column = jnp.broadcast_to(here, (LANES, LANES)).T
        column = jnp.concatenate([column, column], axis=1)
        masks[0, b] = (column == jnp.concatenate([prior, here], axis=1)).astype(F32).astype(BF16)
        masks[1, b] = (column == jnp.concatenate([here, later], axis=1)).astype(F32).astype(BF16)
        return carry

    lax.fori_loop(0, ctxs, one_mask, 0)
    source[pl.ds(0, LANES), :] = jnp.zeros((LANES, LANES), BF16)
    source[pl.ds((ctxs + 1) * LANES, LANES), :] = jnp.zeros((LANES, LANES), BF16)
    group_of_lane = iota((LANES, LANES), 1) // group_size

    def convolve(s):
        way, half = 1 - s // 2, s % 2

        def order(b, carry):
            block = got[s, :, b].astype(F32).reshape(LANES, LANES).astype(BF16)
            at = pl.multiple_of((b + 1) * LANES, LANES)
            source[pl.ds(at, LANES), :] = dot(to_seq[b], block).astype(BF16)
            return carry

        lax.fori_loop(0, ctxs, order, 0)

        def one_tile(b, carry):
            window = source[pl.ds(pl.multiple_of((b + way) * LANES, LANES), 2 * LANES), :]
            mask = masks[way, b]
            total = jnp.zeros((LANES, LANES), F32)
            for g in range(stage_groups):
                band = bands[way, half * stage_groups + g] * mask
                total = jnp.where(group_of_lane == g, dot(band, window), total)
            back = dot(to_arrival[b], total.astype(BF16))
            outgoing[s, :, b] = back.reshape(ctxs, 8, LANES).astype(BF16)
            return carry

        lax.fori_loop(0, ctxs, one_tile, 0)

    def send_final(s):
        half_blocks = ctxs // tps
        for j in range(ctxs):
            target = lax.rem(c + j, ctxs)
            for k in range(tps):
                pltpu.make_async_remote_copy(
                    src_ref=outgoing.at[s, target, pl.ds(k * half_blocks, half_blocks)],
                    dst_ref=final.at[s, t, c],
                    send_sem=final_send.at[s],
                    recv_sem=final_recv.at[s],
                    device_id=(behind, target, k),
                    device_id_type=MESH,
                ).start()

    for s in range(STAGES):
        await_bytes(got.at[s, pl.ds(0, ctxs - 1)], stage_recv.at[s])
        convolve(s)
        send_final(s)
        if s == 0:
            for copy in factor_copies():
                copy.start()

    for copy in factor_copies():
        copy.wait_send()
    await_bytes(factors, factor_recv)

    def finish(s):
        half = s % 2

        def one(i, carry):
            side, peer = i // ctxs, i % ctxs
            near = pl.ds(pl.multiple_of(peer * (2 * LANES) + half * LANES, LANES), LANES)
            far = pl.ds(
                pl.multiple_of(side * (ctxs * 2 * LANES) + peer * (2 * LANES) + half * LANES, LANES),
                LANES,
            )
            conv = final[s, side, peer].astype(F32).reshape(half_rows, LANES)
            if s >= 2:
                out_ref[0, 0, :, far] = (factors[side, 0, :, near].astype(F32) * conv).astype(BF16)
            else:
                out_ref[0, 1, :, far] = (factors[side, 2, :, near].astype(F32) * conv).astype(BF16)
                out_ref[0, 2, :, far] = (factors[side, 1, :, near].astype(F32) * conv).astype(BF16)
            return carry

        lax.fori_loop(0, tps * ctxs, one, 0)

    for s in range(STAGES):
        await_bytes(final.at[s], final_recv.at[s])
        finish(s)

    await_bytes(marks_all.at[pl.ds(0, ctxs - 1)], mark_send)
    for s in range(STAGES):
        await_bytes(stage.at[s, pl.ds(0, ctxs - 1)], stage_send.at[s])
        await_bytes(outgoing.at[s], final_send.at[s])


def shards(sizes, qkv_proj, cotangent, block_dest, doc_start, mr_filter):
    pipes, ctxs, tps = sizes
    rows, channels = cotangent.shape[1:]
    taps = mr_filter.shape[2]
    groups = mr_filter.shape[1] // ctxs
    half_rows = rows // tps
    blocks = rows // 8
    dma = pltpu.SemaphoreType.DMA
    anywhere = pl.BlockSpec(memory_space=pl.ANY)
    vmem = pl.BlockSpec(memory_space=pltpu.VMEM)
    return pl.pallas_call(
        functools.partial(kernel, sizes),
        out_shape=jax.ShapeDtypeStruct((1, 3, half_rows, channels * tps), BF16),
        in_specs=[anywhere, anywhere, vmem, vmem, vmem],
        out_specs=vmem,
        scratch_shapes=[
            pltpu.VMEM((4, rows, channels), BF16),
            pltpu.VMEM((STAGES, ctxs, blocks, 8, LANES), BF16),
            pltpu.VMEM((STAGES, ctxs, blocks, 8, LANES), BF16),
            pltpu.VMEM((ctxs, LANES), jnp.int32),
            pltpu.VMEM((2, groups, 2 * taps), F32),
            pltpu.VMEM((2, groups, taps, 2 * taps), BF16),
            pltpu.VMEM((ctxs, LANES), F32),
            pltpu.VMEM((LANES, LANES), F32),
            pltpu.VMEM((2, ctxs, LANES, 2 * LANES), BF16),
            pltpu.VMEM((ctxs, LANES, LANES), BF16),
            pltpu.VMEM((ctxs, LANES, LANES), BF16),
            pltpu.VMEM(((ctxs + 2) * LANES, LANES), BF16),
            pltpu.VMEM((STAGES, ctxs, blocks, 8, LANES), BF16),
            pltpu.VMEM((STAGES, tps, ctxs, blocks // tps, 8, LANES), BF16),
            pltpu.VMEM((tps, 3, half_rows, channels), BF16),
            dma((4,)),
            dma((STAGES,)),
            dma((STAGES,)),
            dma,
            dma,
            dma,
            dma,
            dma((STAGES,)),
            dma((STAGES,)),
        ],
        compiler_params=pltpu.CompilerParams(
            collective_id=0, has_side_effects=True, vmem_limit_bytes=44 << 20
        ),
        name="hyena_input_grads",
    )(qkv_proj, cotangent, block_dest, doc_start, mr_filter)


def solution(mesh):
    sizes = (mesh.shape["pipe"], mesh.shape["ctx"], mesh.shape["tp"])
    placed = (
        P("pipe", None, "ctx", "tp"),
        P("pipe", "ctx", "tp"),
        P(),
        P("pipe", "ctx"),
        P("pipe", "tp", None),
    )
    return jax.shard_map(
        functools.partial(shards, sizes),
        mesh=mesh,
        in_specs=placed,
        out_specs=P("pipe", None, ("ctx", "tp"), None),
        check_vma=False,
    )
```

```python
import functools

import jax
import jax.numpy as jnp
from jax import lax
from jax.experimental import pallas as pl
from jax.experimental.pallas import tpu as pltpu
from jax.sharding import PartitionSpec as P

MESH = pl.DeviceIdType.MESH
F32 = jnp.float32
BF16 = jnp.bfloat16
LANES = 128
STAGES = 4
RING = 4


def iota(shape, dim):
    return lax.broadcasted_iota(jnp.int32, shape, dim)


def dot(a, b):
    return jnp.dot(a, b, preferred_element_type=F32)


def await_bytes(ref, sem):
    pltpu.make_async_copy(ref, ref, sem).wait()


def kernel(
    sizes,
    qkv_ref,
    cot_ref,
    dest_ref,
    marks_ref,
    filt_ref,
    out_ref,
    raw,
    stage,
    got,
    marks_all,
    taps,
    bands,
    pos_all,
    counts,
    masks,
    to_seq,
    to_arrival,
    source,
    outgoing,
    final,
    returned,
    ready,
    factors,
    dest_here,
    filt_here,
    load_sem,
    stage_send,
    stage_recv,
    mark_send,
    mark_recv,
    factor_send,
    factor_recv,
    final_send,
    final_recv,
    return_send,
    return_recv,
    ready_send,
    ready_recv,
):
    pipes, ctxs, tps = sizes
    p, c, t = lax.axis_index("pipe"), lax.axis_index("ctx"), lax.axis_index("tp")
    behind = lax.rem(p + pipes - 1, pipes)
    ahead = lax.rem(p + 1, pipes)
    rows = raw.shape[1]
    half_rows = rows // tps
    blocks = rows // 8
    half_blocks = half_rows // 8
    groups = taps.shape[1]
    stage_groups = groups // 2
    plane = ctxs // RING
    deep, flat = c // plane, c % plane
    sign = 1 - 2 * t
    half_cols = ctxs * LANES
    plane_cols = plane * LANES
    crossing = pl.ds(pl.multiple_of((1 - t) * half_rows, half_rows), half_rows)
    group_size = LANES // stage_groups

    barrier = pltpu.get_barrier_semaphore()
    for j in range(1, ctxs):
        peer = (p, lax.rem(c + j, ctxs), t)
        pl.semaphore_signal(barrier, inc=1, device_id=peer, device_id_type=MESH)
    for j in range(ctxs):
        for k in range(tps):
            peer = (ahead, lax.rem(c + j, ctxs), k)
            pl.semaphore_signal(barrier, inc=1, device_id=peer, device_id_type=MESH)

    loads = []
    first_group = pl.multiple_of(c * stage_groups, stage_groups)
    for i, (source_ref, target_ref) in enumerate(
        (
            (cot_ref.at[0], raw.at[0]),
            (qkv_ref.at[0, 0], raw.at[1]),
            (qkv_ref.at[0, 1], raw.at[2]),
            (qkv_ref.at[0, 2], raw.at[3]),
            (dest_ref, dest_here),
            (filt_ref.at[0, pl.ds(first_group, stage_groups)], filt_here.at[0]),
            (filt_ref.at[0, pl.ds(ctxs * stage_groups + first_group, stage_groups)], filt_here.at[1]),
            (marks_ref, marks_all.at[pl.ds(c, 1)]),
        )
    ):
        load = pltpu.make_async_copy(source_ref, target_ref, load_sem.at[i])
        load.start()
        loads.append(load)

    def products(s):
        first, second, half = 2 * (s // 2), 2 * (s // 2) + 1, s % 2

        def one(j, carry):
            col = pl.multiple_of(half * half_cols + j * LANES, LANES)
            a = raw[first, :, pl.ds(col, LANES)].astype(F32)
            b = raw[second, :, pl.ds(col, LANES)].astype(F32)
            stage[s, j] = (a * b).reshape(rows // 8, 8, LANES).astype(BF16)
            return carry

        lax.fori_loop(0, ctxs, one, 0)

    def stage_copy(s, j):
        target = lax.rem(c + j, ctxs)
        return pltpu.make_async_remote_copy(
            src_ref=stage.at[s, target],
            dst_ref=got.at[s, c],
            send_sem=stage_send.at[s],
            recv_sem=stage_recv.at[s],
            device_id=(p, target, t),
            device_id_type=MESH,
        )

    def send_stage(s):
        for j in range(1, ctxs):
            stage_copy(s, j).start()
        got[s, c] = stage[s, c]

    loads[0].wait()
    loads[1].wait()
    products(0)
    pl.semaphore_wait(barrier, ctxs - 1 + ctxs * tps)
    for j in range(1, ctxs):
        pltpu.make_async_remote_copy(
            src_ref=marks_ref,
            dst_ref=marks_all.at[pl.ds(c, 1)],
            send_sem=mark_send,
            recv_sem=mark_recv,
            device_id=(p, lax.rem(c + j, ctxs), t),
            device_id_type=MESH,
        ).start()
    send_stage(0)
    products(1)
    send_stage(1)
    loads[2].wait()
    loads[3].wait()
    products(2)
    send_stage(2)
    products(3)
    send_stage(3)

    arrays = (cot_ref.at[0], qkv_ref.at[0, 1], qkv_ref.at[0, 2])

    def near_factors():
        span = pl.ds(pl.multiple_of(t * half_rows, half_rows), half_rows)
        return [
            pltpu.make_async_remote_copy(
                src_ref=ref.at[span],
                dst_ref=factors.at[t, i],
                send_sem=factor_send.at[0],
                recv_sem=factor_recv.at[0],
                device_id=(behind, c, t),
                device_id_type=MESH,
            )
            for i, ref in enumerate(arrays)
        ]

    def owner_depth(side_sign, step):
        return lax.rem(deep - side_sign * step + RING, RING)

    def far_factors():
        copies = []
        for step in range(RING // 2, RING):
            for half in range(2):
                col = half * half_cols + owner_depth(sign, step) * plane_cols
                span = pl.ds(pl.multiple_of(col, plane_cols), plane_cols)
                for i, ref in enumerate(arrays):
                    copies.append(
                        pltpu.make_async_remote_copy(
                            src_ref=ref.at[crossing, span],
                            dst_ref=factors.at[t, i, :, span],
                            send_sem=factor_send.at[1],
                            recv_sem=factor_recv.at[1],
                            device_id=(behind, c, 1 - t),
                            device_id_type=MESH,
                        )
                    )
        return copies

    for load in loads[4:]:
        load.wait()
    mine = filt_here[...].astype(F32).reshape(groups, LANES).astype(BF16)
    lag, lane = iota((LANES, 2 * LANES), 0), iota((LANES, 2 * LANES), 1)
    taps[0] = dot(mine, (lane == LANES - lag).astype(BF16))
    taps[1] = dot(mine, (lane == lag).astype(BF16))

    def one_band(i, carry):
        for way in range(2):
            row = jnp.broadcast_to(taps[way, pl.ds(i, 1), :], (LANES, 2 * LANES))
            band = pltpu.roll(row, 0, 1, stride=1, stride_axis=0)
            bands[way, i] = band.astype(BF16)
        return carry

    lax.fori_loop(0, groups, one_band, 0)

    slots = ctxs * ctxs
    dest = jnp.broadcast_to(dest_here[pl.ds(p, 1), :], (ctxs, slots))
    entry, tile = iota((ctxs, slots), 1), iota((ctxs, slots), 0)
    slot = jnp.where(entry % ctxs == tile, dest - tile * ctxs, 0).astype(F32).astype(BF16)
    spread = (iota((slots, LANES), 0) // ctxs == iota((slots, LANES), 1) // 8).astype(BF16)
    pos_all[...] = dot(slot, spread) * 8.0 + (iota((ctxs, LANES), 1) % 8).astype(F32)

    await_bytes(marks_all.at[pl.ds(0, ctxs - 1)], mark_recv)
    down = iota((LANES, LANES), 0)
    across = iota((LANES, LANES), 1)
    owner = iota((ctxs, LANES), 0) == iota((ctxs, LANES), 1) // 8

    def one_order(b, table):
        pick = (down == b * 8 + across % 8).astype(BF16)
        marks = dot(marks_all[...].astype(F32).astype(BF16), pick)
        marks = jnp.sum(jnp.where(owner, marks, 0.0), axis=0, keepdims=True)
        pos = pos_all[pl.ds(b, 1), :]
        rank = down.astype(F32)
        place = (pos == rank).astype(F32)
        to_seq[b] = place.astype(BF16)
        to_arrival[b] = place.T.astype(BF16)
        count = jnp.sum(jnp.where(pos <= rank, marks, 0.0), axis=1, keepdims=True)
        return jnp.where(across == b, count, table)

    table = lax.fori_loop(0, ctxs, one_order, jnp.zeros((LANES, LANES), F32))
    counts[...] = table.T

    def one_mask(b, carry):
        here = counts[pl.ds(b, 1), :]
        total = here[:, LANES - 1 :]
        prior = counts[pl.ds(jnp.maximum(b - 1, 0), 1), :]
        prior = jnp.where(b > 0, prior - prior[:, LANES - 1 :], -1.0)
        later = counts[pl.ds(jnp.minimum(b + 1, ctxs - 1), 1), :]
        later = jnp.where(b < ctxs - 1, later + total, -1.0)
        column = jnp.broadcast_to(here, (LANES, LANES)).T
        column = jnp.concatenate([column, column], axis=1)
        masks[0, b] = (column == jnp.concatenate([prior, here], axis=1)).astype(F32).astype(BF16)
        masks[1, b] = (column == jnp.concatenate([here, later], axis=1)).astype(F32).astype(BF16)
        return carry

    lax.fori_loop(0, ctxs, one_mask, 0)
    source[pl.ds(0, LANES), :] = jnp.zeros((LANES, LANES), BF16)
    source[pl.ds((ctxs + 1) * LANES, LANES), :] = jnp.zeros((LANES, LANES), BF16)
    group_of_lane = iota((LANES, LANES), 1) // group_size

    def convolve(s):
        way, half = 1 - s // 2, s % 2

        def order(b, carry):
            block = got[s, :, b].astype(F32).reshape(LANES, LANES).astype(BF16)
            at = pl.multiple_of((b + 1) * LANES, LANES)
            source[pl.ds(at, LANES), :] = dot(to_seq[b], block).astype(BF16)
            return carry

        lax.fori_loop(0, ctxs, order, 0)

        def one_tile(b, carry):
            window = source[pl.ds(pl.multiple_of((b + way) * LANES, LANES), 2 * LANES), :]
            mask = masks[way, b]
            total = jnp.zeros((LANES, LANES), F32)
            for g in range(stage_groups):
                band = bands[way, half * stage_groups + g] * mask
                total = jnp.where(group_of_lane == g, dot(band, window), total)
            back = dot(to_arrival[b], total.astype(BF16))
            outgoing[s, :, b] = back.reshape(ctxs, 8, LANES).astype(BF16)
            return carry

        lax.fori_loop(0, ctxs, one_tile, 0)

    def send_final(s):
        for step in range(RING // 2):
            for k in range(plane):
                y = lax.rem(flat + k, plane)
                target = lax.rem(deep + sign * step + RING, RING) * plane + y
                piece = outgoing.at[s, target, pl.ds((1 - t) * half_blocks, half_blocks)]
                if step == 0 and k == 0:
                    returned[s, step * plane + flat] = outgoing[s, c, pl.ds((1 - t) * half_blocks, half_blocks)]
                else:
                    pltpu.make_async_remote_copy(
                        src_ref=piece,
                        dst_ref=returned.at[s, step * plane + flat],
                        send_sem=return_send.at[s],
                        recv_sem=return_recv.at[s],
                        device_id=(p, target, t),
                        device_id_type=MESH,
                    ).start()
        for step in range(RING):
            for k in range(plane):
                y = lax.rem(flat + k, plane)
                target = lax.rem(deep + sign * step + RING, RING) * plane + y
                for side in (t, 1 - t) if step >= RING // 2 else (t,):
                    pltpu.make_async_remote_copy(
                        src_ref=outgoing.at[s, target, pl.ds(side * half_blocks, half_blocks)],
                        dst_ref=final.at[s, t * ctxs + c],
                        send_sem=final_send.at[s],
                        recv_sem=final_recv.at[s],
                        device_id=(behind, target, side),
                        device_id_type=MESH,
                    ).start()

    def outputs(s):
        return ((0, 0, 0),) if s >= 2 else ((1, 2, 3), (2, 1, 2))

    def ready_copies(s):
        half = s % 2
        copies = []
        for step in range(RING // 2):
            col = half * half_cols + owner_depth(sign, step) * plane_cols
            span = pl.ds(pl.multiple_of(t * 2 * half_cols + col, plane_cols), plane_cols)
            for out, _, _ in outputs(s):
                copies.append(
                    pltpu.make_async_remote_copy(
                        src_ref=ready.at[half, step, out],
                        dst_ref=out_ref.at[0, out, :, span],
                        send_sem=ready_send,
                        recv_sem=ready_recv,
                        device_id=(behind, c, 1 - t),
                        device_id_type=MESH,
                    )
                )
        return copies

    def pass_on(s):
        half = s % 2
        await_bytes(returned.at[s, pl.ds(0, ctxs // 2 - 1)], return_recv.at[s])
        for step in range(RING // 2):

            def one(y, carry):
                col = half * half_cols + owner_depth(sign, step) * plane_cols + y * LANES
                near = pl.ds(pl.multiple_of(col, LANES), LANES)
                at = pl.ds(pl.multiple_of(y * LANES, LANES), LANES)
                conv = returned[s, step * plane + y].astype(F32).reshape(half_rows, LANES)
                for out, _, factor in outputs(s):
                    value = raw[factor, crossing, near].astype(F32)
                    ready[half, step, out, :, at] = (value * conv).astype(BF16)
                return carry

            lax.fori_loop(0, plane, one, 0)
        for copy in ready_copies(s):
            copy.start()

    for copy in near_factors():
        copy.start()
    for s in range(STAGES):
        await_bytes(got.at[s, pl.ds(0, ctxs - 1)], stage_recv.at[s])
        convolve(s)
        send_final(s)
        if s == 0:
            for copy in far_factors():
                copy.start()
        if s >= 1:
            pass_on(s - 1)
    pass_on(STAGES - 1)

    await_bytes(factors.at[0], factor_recv.at[0])
    await_bytes(factors.at[0, :, :, pl.ds(0, half_cols)], factor_recv.at[1])

    def finish(s):
        half = s % 2

        def one(side, depth, y):
            col = half * half_cols + depth * plane_cols + y * LANES
            near = pl.ds(pl.multiple_of(col, LANES), LANES)
            far = pl.ds(pl.multiple_of(side * 2 * half_cols + col, LANES), LANES)
            conv = final[s, side * ctxs + depth * plane + y].astype(F32).reshape(half_rows, LANES)
            for out, factor, _ in outputs(s):
                value = factors[side, factor, :, near].astype(F32)
                out_ref[0, out, :, far] = (value * conv).astype(BF16)

        def own(i, carry):
            one(t, i // plane, i % plane)
            return carry

        lax.fori_loop(0, ctxs, own, 0)

        def other(i, carry):
            one(1 - t, owner_depth(-sign, RING // 2 + i // plane), i % plane)
            return carry

        lax.fori_loop(0, ctxs // 2, other, 0)

    for s in range(STAGES):
        await_bytes(final.at[s, pl.ds(0, ctxs + ctxs // 2)], final_recv.at[s])
        finish(s)
    await_bytes(out_ref.at[0, :, :, pl.ds(0, half_cols)], ready_recv)

    await_bytes(marks_all.at[pl.ds(0, ctxs - 1)], mark_send)
    for s in range(STAGES):
        await_bytes(stage.at[s, pl.ds(0, ctxs - 1)], stage_send.at[s])
        await_bytes(returned.at[s, pl.ds(0, ctxs // 2 - 1)], return_send.at[s])
        await_bytes(final.at[s, pl.ds(0, ctxs + ctxs // 2)], final_send.at[s])
    await_bytes(factors.at[0], factor_send.at[0])
    await_bytes(factors.at[0, :, :, pl.ds(0, half_cols)], factor_send.at[1])
    await_bytes(out_ref.at[0, :, :, pl.ds(0, half_cols)], ready_send)


def shards(sizes, qkv_proj, cotangent, block_dest, doc_start, mr_filter):
    pipes, ctxs, tps = sizes
    rows, channels = cotangent.shape[1:]
    taps = mr_filter.shape[2]
    groups = mr_filter.shape[1] // ctxs
    half_rows = rows // tps
    blocks = rows // 8
    dma = pltpu.SemaphoreType.DMA
    return pl.pallas_call(
        functools.partial(kernel, sizes),
        out_shape=jax.ShapeDtypeStruct((1, 3, half_rows, channels * tps), BF16),
        in_specs=[pl.BlockSpec(memory_space=pltpu.HBM)] * 5,
        out_specs=pl.BlockSpec(memory_space=pltpu.VMEM),
        scratch_shapes=[
            pltpu.VMEM((4, rows, channels), BF16),
            pltpu.VMEM((STAGES, ctxs, blocks, 8, LANES), BF16),
            pltpu.VMEM((STAGES, ctxs, blocks, 8, LANES), BF16),
            pltpu.VMEM((ctxs, LANES), jnp.int32),
            pltpu.VMEM((2, groups, 2 * taps), F32),
            pltpu.VMEM((2, groups, taps, 2 * taps), BF16),
            pltpu.VMEM((ctxs, LANES), F32),
            pltpu.VMEM((LANES, LANES), F32),
            pltpu.VMEM((2, ctxs, LANES, 2 * LANES), BF16),
            pltpu.VMEM((ctxs, LANES, LANES), BF16),
            pltpu.VMEM((ctxs, LANES, LANES), BF16),
            pltpu.VMEM(((ctxs + 2) * LANES, LANES), BF16),
            pltpu.VMEM((STAGES, ctxs, blocks, 8, LANES), BF16),
            pltpu.VMEM((STAGES, tps * ctxs, blocks // tps, 8, LANES), BF16),
            pltpu.VMEM((STAGES, ctxs // 2, blocks // tps, 8, LANES), BF16),
            pltpu.VMEM((2, RING // 2, 3, half_rows, ctxs // RING * LANES), BF16),
            pltpu.VMEM((tps, 3, half_rows, channels), BF16),
            pltpu.VMEM(block_dest.shape, jnp.int32),
            pltpu.VMEM((2, groups // 2, taps), BF16),
            dma((8,)),
            dma((STAGES,)),
            dma((STAGES,)),
            dma,
            dma,
            dma((2,)),
            dma((2,)),
            dma((STAGES,)),
            dma((STAGES,)),
            dma((STAGES,)),
            dma((STAGES,)),
            dma,
            dma,
        ],
        compiler_params=pltpu.CompilerParams(
            collective_id=0, has_side_effects=True, vmem_limit_bytes=44 << 20
        ),
        name="hyena_input_grads",
    )(*(pltpu.with_memory_space_constraint(x, pltpu.HBM) for x in (qkv_proj, cotangent, block_dest, doc_start, mr_filter)))


def solution(mesh):
    sizes = (mesh.shape["pipe"], mesh.shape["ctx"], mesh.shape["tp"])
    placed = (
        P("pipe", None, "ctx", "tp"),
        P("pipe", "ctx", "tp"),
        P(),
        P("pipe", "ctx"),
        P("pipe", "tp", None),
    )
    return jax.shard_map(
        functools.partial(shards, sizes),
        mesh=mesh,
        in_specs=placed,
        out_specs=P("pipe", None, ("ctx", "tp"), None),
        check_vma=False,
    )
```

```python
import functools

import jax
import jax.numpy as jnp
from jax import lax
from jax.experimental import pallas as pl
from jax.experimental.pallas import tpu as pltpu
from jax.sharding import PartitionSpec as P

MESH = pl.DeviceIdType.MESH
F32 = jnp.float32
BF16 = jnp.bfloat16
LANES = 128
STAGES = 4
RING = 4


def iota(shape, dim):
    return lax.broadcasted_iota(jnp.int32, shape, dim)


def dot(a, b):
    return jnp.dot(a, b, preferred_element_type=F32)


def await_bytes(ref, sem):
    pltpu.make_async_copy(ref, ref, sem).wait()


def kernel(
    sizes,
    qkv_ref,
    cot_ref,
    dest_ref,
    marks_ref,
    filt_ref,
    out_ref,
    raw,
    stage,
    got,
    marks_all,
    taps,
    bands,
    pos_all,
    counts,
    masks,
    to_seq,
    to_arrival,
    source,
    outgoing,
    final,
    returned,
    ready,
    relay,
    factors,
    dest_here,
    filt_here,
    load_sem,
    stage_send,
    stage_recv,
    mark_send,
    mark_recv,
    factor_send,
    factor_recv,
    final_send,
    final_recv,
    return_send,
    return_recv,
    ready_send,
    ready_recv,
    relay_send,
    relay_recv,
    forward_send,
):
    pipes, ctxs, tps = sizes
    p, c, t = lax.axis_index("pipe"), lax.axis_index("ctx"), lax.axis_index("tp")
    behind = lax.rem(p + pipes - 1, pipes)
    ahead = lax.rem(p + 1, pipes)
    rows = raw.shape[1]
    half_rows = rows // tps
    blocks = rows // 8
    half_blocks = half_rows // 8
    groups = taps.shape[1]
    stage_groups = groups // 2
    plane = ctxs // RING
    deep, flat = c // plane, c % plane
    sign = 1 - 2 * t
    half_cols = ctxs * LANES
    plane_cols = plane * LANES
    crossing = pl.ds(pl.multiple_of((1 - t) * half_rows, half_rows), half_rows)
    group_size = LANES // stage_groups

    barrier = pltpu.get_barrier_semaphore()
    for j in range(1, ctxs):
        peer = (p, lax.rem(c + j, ctxs), t)
        pl.semaphore_signal(barrier, inc=1, device_id=peer, device_id_type=MESH)
    for j in range(ctxs):
        for k in range(tps):
            peer = (ahead, lax.rem(c + j, ctxs), k)
            pl.semaphore_signal(barrier, inc=1, device_id=peer, device_id_type=MESH)
        peer = (behind, lax.rem(c + j, ctxs), 1 - t)
        pl.semaphore_signal(barrier, inc=1, device_id=peer, device_id_type=MESH)

    loads = []
    first_group = pl.multiple_of(c * stage_groups, stage_groups)
    for i, (source_ref, target_ref) in enumerate(
        (
            (cot_ref.at[0], raw.at[0]),
            (qkv_ref.at[0, 0], raw.at[1]),
            (qkv_ref.at[0, 1], raw.at[2]),
            (qkv_ref.at[0, 2], raw.at[3]),
            (dest_ref, dest_here),
            (filt_ref.at[0, pl.ds(first_group, stage_groups)], filt_here.at[0]),
            (filt_ref.at[0, pl.ds(ctxs * stage_groups + first_group, stage_groups)], filt_here.at[1]),
            (marks_ref, marks_all.at[pl.ds(c, 1)]),
        )
    ):
        load = pltpu.make_async_copy(source_ref, target_ref, load_sem.at[i])
        load.start()
        loads.append(load)

    def products(s):
        first, second, half = 2 * (s // 2), 2 * (s // 2) + 1, s % 2

        def one(j, carry):
            col = pl.multiple_of(half * half_cols + j * LANES, LANES)
            a = raw[first, :, pl.ds(col, LANES)].astype(F32)
            b = raw[second, :, pl.ds(col, LANES)].astype(F32)
            stage[s, j] = (a * b).reshape(rows // 8, 8, LANES).astype(BF16)
            return carry

        lax.fori_loop(0, ctxs, one, 0)

    def owner_depth(side_sign, step):
        return lax.rem(deep - side_sign * step + RING, RING)

    def half_span(side):
        return pl.ds(side * half_blocks, half_blocks)

    def send_stage(s):
        if s < 2:
            for step in range(RING // 2, RING):
                span = pl.ds(owner_depth(sign, step) * plane, plane)
                pltpu.make_async_remote_copy(
                    src_ref=stage.at[s, span, half_span(1 - t)],
                    dst_ref=relay.at[s, step - RING // 2],
                    send_sem=relay_send,
                    recv_sem=relay_recv.at[s],
                    device_id=(behind, c, 1 - t),
                    device_id_type=MESH,
                ).start()
        for step in range(RING):
            for k in range(plane):
                target = owner_depth(sign, step) * plane + lax.rem(flat + k, plane)
                piece, place = stage.at[s, target], got.at[s, c]
                if step >= RING // 2:
                    piece, place = piece.at[half_span(t)], place.at[half_span(t)]
                if step > 0 or k > 0:
                    pltpu.make_async_remote_copy(
                        src_ref=piece,
                        dst_ref=place,
                        send_sem=stage_send.at[s],
                        recv_sem=stage_recv.at[s],
                        device_id=(p, target, t),
                        device_id_type=MESH,
                    ).start()
        got[s, c] = stage[s, c]

    def forward(s):
        for step in range(RING // 2, RING):
            depth = owner_depth(-sign, step)
            if s >= 2:

                def one(y, carry):
                    near = pl.ds(
                        pl.multiple_of(s % 2 * half_cols + depth * plane_cols + y * LANES, LANES),
                        LANES,
                    )
                    key = factors[1 - t, 1, :, near].astype(F32)
                    value = factors[1 - t, 2, :, near].astype(F32)
                    mixed = (key * value).reshape(half_blocks, 8, LANES)
                    relay[s, step - RING // 2, y] = mixed.astype(BF16)
                    return carry

                lax.fori_loop(0, plane, one, 0)
            for k in range(plane):
                y = lax.rem(flat + k, plane)
                pltpu.make_async_remote_copy(
                    src_ref=relay.at[s, step - RING // 2, y],
                    dst_ref=got.at[s, c, half_span(t)],
                    send_sem=forward_send,
                    recv_sem=stage_recv.at[s],
                    device_id=(ahead, depth * plane + y, 1 - t),
                    device_id_type=MESH,
                ).start()

    arrays = (cot_ref.at[0], qkv_ref.at[0, 1], qkv_ref.at[0, 2])

    def near_factors():
        span = pl.ds(pl.multiple_of(t * half_rows, half_rows), half_rows)
        return [
            pltpu.make_async_remote_copy(
                src_ref=ref.at[span],
                dst_ref=factors.at[t, i],
                send_sem=factor_send.at[2],
                recv_sem=factor_recv.at[2],
                device_id=(behind, c, t),
                device_id_type=MESH,
            )
            for i, ref in enumerate(arrays)
        ]

    def far_factors(part):
        copies = []
        for half in range(2):
            for step in range(RING // 2, RING):
                col = half * half_cols + owner_depth(sign, step) * plane_cols
                span = pl.ds(pl.multiple_of(col, plane_cols), plane_cols)
                for i in part:
                    copies.append(
                        pltpu.make_async_remote_copy(
                            src_ref=arrays[i].at[crossing, span],
                            dst_ref=factors.at[t, i, :, span],
                            send_sem=factor_send.at[min(i, 1)],
                            recv_sem=factor_recv.at[min(i, 1)],
                            device_id=(behind, c, 1 - t),
                            device_id_type=MESH,
                        )
                    )
        return copies

    pl.semaphore_wait(barrier, ctxs - 1 + ctxs * tps + ctxs)
    for copy in far_factors((1, 2)):
        copy.start()
    loads[0].wait()
    loads[1].wait()
    products(0)
    for j in range(1, ctxs):
        pltpu.make_async_remote_copy(
            src_ref=marks_ref,
            dst_ref=marks_all.at[pl.ds(c, 1)],
            send_sem=mark_send,
            recv_sem=mark_recv,
            device_id=(p, lax.rem(c + j, ctxs), t),
            device_id_type=MESH,
        ).start()
    send_stage(0)
    products(1)
    send_stage(1)
    loads[2].wait()
    loads[3].wait()
    products(2)
    send_stage(2)
    products(3)
    send_stage(3)
    for copy in far_factors((0,)) + near_factors():
        copy.start()

    for load in loads[4:]:
        load.wait()
    mine = filt_here[...].astype(F32).reshape(groups, LANES).astype(BF16)
    lag, lane = iota((LANES, 2 * LANES), 0), iota((LANES, 2 * LANES), 1)
    taps[0] = dot(mine, (lane == LANES - lag).astype(BF16))
    taps[1] = dot(mine, (lane == lag).astype(BF16))

    def one_band(i, carry):
        for way in range(2):
            row = jnp.broadcast_to(taps[way, pl.ds(i, 1), :], (LANES, 2 * LANES))
            band = pltpu.roll(row, 0, 1, stride=1, stride_axis=0)
            bands[way, i] = band.astype(BF16)
        return carry

    lax.fori_loop(0, groups, one_band, 0)

    for s in range(2):
        await_bytes(relay.at[s], relay_recv.at[s])
        forward(s)

    slots = ctxs * ctxs
    dest = jnp.broadcast_to(dest_here[pl.ds(p, 1), :], (ctxs, slots))
    entry, tile = iota((ctxs, slots), 1), iota((ctxs, slots), 0)
    slot = jnp.where(entry % ctxs == tile, dest - tile * ctxs, 0).astype(F32).astype(BF16)
    spread = (iota((slots, LANES), 0) // ctxs == iota((slots, LANES), 1) // 8).astype(BF16)
    pos_all[...] = dot(slot, spread) * 8.0 + (iota((ctxs, LANES), 1) % 8).astype(F32)

    await_bytes(marks_all.at[pl.ds(0, ctxs - 1)], mark_recv)
    down = iota((LANES, LANES), 0)
    across = iota((LANES, LANES), 1)
    owner = iota((ctxs, LANES), 0) == iota((ctxs, LANES), 1) // 8

    def one_order(b, table):
        pick = (down == b * 8 + across % 8).astype(BF16)
        marks = dot(marks_all[...].astype(F32).astype(BF16), pick)
        marks = jnp.sum(jnp.where(owner, marks, 0.0), axis=0, keepdims=True)
        pos = pos_all[pl.ds(b, 1), :]
        rank = down.astype(F32)
        place = (pos == rank).astype(F32)
        to_seq[b] = place.astype(BF16)
        to_arrival[b] = place.T.astype(BF16)
        count = jnp.sum(jnp.where(pos <= rank, marks, 0.0), axis=1, keepdims=True)
        return jnp.where(across == b, count, table)

    table = lax.fori_loop(0, ctxs, one_order, jnp.zeros((LANES, LANES), F32))
    counts[...] = table.T

    def one_mask(b, carry):
        here = counts[pl.ds(b, 1), :]
        total = here[:, LANES - 1 :]
        prior = counts[pl.ds(jnp.maximum(b - 1, 0), 1), :]
        prior = jnp.where(b > 0, prior - prior[:, LANES - 1 :], -1.0)
        later = counts[pl.ds(jnp.minimum(b + 1, ctxs - 1), 1), :]
        later = jnp.where(b < ctxs - 1, later + total, -1.0)
        column = jnp.broadcast_to(here, (LANES, LANES)).T
        column = jnp.concatenate([column, column], axis=1)
        masks[0, b] = (column == jnp.concatenate([prior, here], axis=1)).astype(F32).astype(BF16)
        masks[1, b] = (column == jnp.concatenate([here, later], axis=1)).astype(F32).astype(BF16)
        return carry

    lax.fori_loop(0, ctxs, one_mask, 0)
    source[pl.ds(0, LANES), :] = jnp.zeros((LANES, LANES), BF16)
    source[pl.ds((ctxs + 1) * LANES, LANES), :] = jnp.zeros((LANES, LANES), BF16)
    group_of_lane = iota((LANES, LANES), 1) // group_size

    def convolve(s):
        way, half = 1 - s // 2, s % 2

        def order(b, carry):
            block = got[s, :, b].astype(F32).reshape(LANES, LANES).astype(BF16)
            at = pl.multiple_of((b + 1) * LANES, LANES)
            source[pl.ds(at, LANES), :] = dot(to_seq[b], block).astype(BF16)
            return carry

        lax.fori_loop(0, ctxs, order, 0, unroll=8)

        def one_tile(b, carry):
            window = source[pl.ds(pl.multiple_of((b + way) * LANES, LANES), 2 * LANES), :]
            mask = masks[way, b]
            total = jnp.zeros((LANES, LANES), F32)
            for g in range(stage_groups):
                band = bands[way, half * stage_groups + g] * mask
                total = jnp.where(group_of_lane == g, dot(band, window), total)
            back = dot(to_arrival[b], total.astype(BF16))
            outgoing[s, :, b] = back.reshape(ctxs, 8, LANES).astype(BF16)
            return carry

        lax.fori_loop(0, ctxs, one_tile, 0, unroll=4)

    def send_final(s):
        for step in range(RING // 2):
            for k in range(plane):
                y = lax.rem(flat + k, plane)
                target = lax.rem(deep + sign * step + RING, RING) * plane + y
                piece = outgoing.at[s, target, pl.ds((1 - t) * half_blocks, half_blocks)]
                if step == 0 and k == 0:
                    returned[s, step * plane + flat] = outgoing[s, c, pl.ds((1 - t) * half_blocks, half_blocks)]
                else:
                    pltpu.make_async_remote_copy(
                        src_ref=piece,
                        dst_ref=returned.at[s, step * plane + flat],
                        send_sem=return_send.at[s],
                        recv_sem=return_recv.at[s],
                        device_id=(p, target, t),
                        device_id_type=MESH,
                    ).start()
        for step in range(RING):
            for k in range(plane):
                y = lax.rem(flat + k, plane)
                target = lax.rem(deep + sign * step + RING, RING) * plane + y
                for side in (t, 1 - t) if step >= RING // 2 else (t,):
                    pltpu.make_async_remote_copy(
                        src_ref=outgoing.at[s, target, pl.ds(side * half_blocks, half_blocks)],
                        dst_ref=final.at[s, t * ctxs + c],
                        send_sem=final_send.at[s],
                        recv_sem=final_recv.at[s],
                        device_id=(behind, target, side),
                        device_id_type=MESH,
                    ).start()

    def outputs(s):
        return ((0, 0, 0),) if s >= 2 else ((1, 2, 3), (2, 1, 2))

    def ready_copies(s):
        half = s % 2
        copies = []
        for step in range(RING // 2):
            col = half * half_cols + owner_depth(sign, step) * plane_cols
            span = pl.ds(pl.multiple_of(t * 2 * half_cols + col, plane_cols), plane_cols)
            for out, _, _ in outputs(s):
                copies.append(
                    pltpu.make_async_remote_copy(
                        src_ref=ready.at[half, step, out],
                        dst_ref=out_ref.at[0, out, :, span],
                        send_sem=ready_send,
                        recv_sem=ready_recv,
                        device_id=(behind, c, 1 - t),
                        device_id_type=MESH,
                    )
                )
        return copies

    def pass_on(s):
        half = s % 2
        await_bytes(returned.at[s, pl.ds(0, ctxs // 2 - 1)], return_recv.at[s])
        for step in range(RING // 2):

            def one(y, carry):
                col = half * half_cols + owner_depth(sign, step) * plane_cols + y * LANES
                near = pl.ds(pl.multiple_of(col, LANES), LANES)
                at = pl.ds(pl.multiple_of(y * LANES, LANES), LANES)
                conv = returned[s, step * plane + y].astype(F32).reshape(half_rows, LANES)
                for out, _, factor in outputs(s):
                    value = raw[factor, crossing, near].astype(F32)
                    ready[half, step, out, :, at] = (value * conv).astype(BF16)
                return carry

            lax.fori_loop(0, plane, one, 0)
        for copy in ready_copies(s):
            copy.start()

    await_bytes(factors.at[0, pl.ds(0, 2), :, pl.ds(0, half_cols)], factor_recv.at[1])
    forward(2)
    forward(3)
    for s in range(STAGES):
        await_bytes(got.at[s, pl.ds(0, ctxs - 1)], stage_recv.at[s])
        convolve(s)
        send_final(s)
        if s >= 1:
            pass_on(s - 1)
    pass_on(STAGES - 1)

    await_bytes(factors.at[0], factor_recv.at[2])
    await_bytes(factors.at[0, 0, :, pl.ds(0, half_cols)], factor_recv.at[0])

    def finish(s):
        half = s % 2

        def one(side, depth, y):
            col = half * half_cols + depth * plane_cols + y * LANES
            near = pl.ds(pl.multiple_of(col, LANES), LANES)
            far = pl.ds(pl.multiple_of(side * 2 * half_cols + col, LANES), LANES)
            conv = final[s, side * ctxs + depth * plane + y].astype(F32).reshape(half_rows, LANES)
            for out, factor, _ in outputs(s):
                value = factors[side, factor, :, near].astype(F32)
                out_ref[0, out, :, far] = (value * conv).astype(BF16)

        def own(i, carry):
            one(t, i // plane, i % plane)
            return carry

        lax.fori_loop(0, ctxs, own, 0)

        def other(i, carry):
            one(1 - t, owner_depth(-sign, RING // 2 + i // plane), i % plane)
            return carry

        lax.fori_loop(0, ctxs // 2, other, 0)

    for s in range(STAGES):
        await_bytes(final.at[s, pl.ds(0, ctxs + ctxs // 2)], final_recv.at[s])
        finish(s)
    await_bytes(out_ref.at[0, :, :, pl.ds(0, half_cols)], ready_recv)

    await_bytes(marks_all.at[pl.ds(0, ctxs - 1)], mark_send)
    for s in range(STAGES):
        await_bytes(stage.at[s, pl.ds(0, 3 * ctxs // 4 - 1)], stage_send.at[s])
        await_bytes(returned.at[s, pl.ds(0, ctxs // 2 - 1)], return_send.at[s])
        await_bytes(final.at[s, pl.ds(0, ctxs + ctxs // 2)], final_send.at[s])
    await_bytes(factors.at[0], factor_send.at[2])
    await_bytes(factors.at[0, pl.ds(0, 2), :, pl.ds(0, half_cols)], factor_send.at[1])
    await_bytes(relay.at[pl.ds(0, 2)], relay_send)
    await_bytes(relay, forward_send)
    await_bytes(factors.at[0, 0, :, pl.ds(0, half_cols)], factor_send.at[0])
    await_bytes(out_ref.at[0, :, :, pl.ds(0, half_cols)], ready_send)


def shards(sizes, qkv_proj, cotangent, block_dest, doc_start, mr_filter):
    pipes, ctxs, tps = sizes
    rows, channels = cotangent.shape[1:]
    taps = mr_filter.shape[2]
    groups = mr_filter.shape[1] // ctxs
    half_rows = rows // tps
    blocks = rows // 8
    dma = pltpu.SemaphoreType.DMA
    return pl.pallas_call(
        functools.partial(kernel, sizes),
        out_shape=jax.ShapeDtypeStruct((1, 3, half_rows, channels * tps), BF16),
        in_specs=[pl.BlockSpec(memory_space=pltpu.HBM)] * 5,
        out_specs=pl.BlockSpec(memory_space=pltpu.VMEM),
        scratch_shapes=[
            pltpu.VMEM((4, rows, channels), BF16),
            pltpu.VMEM((STAGES, ctxs, blocks, 8, LANES), BF16),
            pltpu.VMEM((STAGES, ctxs, blocks, 8, LANES), BF16),
            pltpu.VMEM((ctxs, LANES), jnp.int32),
            pltpu.VMEM((2, groups, 2 * taps), F32),
            pltpu.VMEM((2, groups, taps, 2 * taps), BF16),
            pltpu.VMEM((ctxs, LANES), F32),
            pltpu.VMEM((LANES, LANES), F32),
            pltpu.VMEM((2, ctxs, LANES, 2 * LANES), BF16),
            pltpu.VMEM((ctxs, LANES, LANES), BF16),
            pltpu.VMEM((ctxs, LANES, LANES), BF16),
            pltpu.VMEM(((ctxs + 2) * LANES, LANES), BF16),
            pltpu.VMEM((STAGES, ctxs, blocks, 8, LANES), BF16),
            pltpu.VMEM((STAGES, tps * ctxs, blocks // tps, 8, LANES), BF16),
            pltpu.VMEM((STAGES, ctxs // 2, blocks // tps, 8, LANES), BF16),
            pltpu.VMEM((2, RING // 2, 3, half_rows, ctxs // RING * LANES), BF16),
            pltpu.VMEM((STAGES, RING // 2, ctxs // RING, blocks // tps, 8, LANES), BF16),
            pltpu.VMEM((tps, 3, half_rows, channels), BF16),
            pltpu.VMEM(block_dest.shape, jnp.int32),
            pltpu.VMEM((2, groups // 2, taps), BF16),
            dma((8,)),
            dma((STAGES,)),
            dma((STAGES,)),
            dma,
            dma,
            dma((3,)),
            dma((3,)),
            dma((STAGES,)),
            dma((STAGES,)),
            dma((STAGES,)),
            dma((STAGES,)),
            dma,
            dma,
            dma,
            dma((2,)),
            dma,
        ],
        compiler_params=pltpu.CompilerParams(
            collective_id=0, has_side_effects=True, vmem_limit_bytes=44 << 20
        ),
        name="hyena_input_grads",
    )(*(pltpu.with_memory_space_constraint(x, pltpu.HBM) for x in (qkv_proj, cotangent, block_dest, doc_start, mr_filter)))


def solution(mesh):
    sizes = (mesh.shape["pipe"], mesh.shape["ctx"], mesh.shape["tp"])
    placed = (
        P("pipe", None, "ctx", "tp"),
        P("pipe", "ctx", "tp"),
        P(),
        P("pipe", "ctx"),
        P("pipe", "tp", None),
    )
    return jax.shard_map(
        functools.partial(shards, sizes),
        mesh=mesh,
        in_specs=placed,
        out_specs=P("pipe", None, ("ctx", "tp"), None),
        check_vma=False,
    )
```

```python
import functools

import jax
import jax.numpy as jnp
from jax import lax
from jax.experimental import pallas as pl
from jax.experimental.pallas import tpu as pltpu
from jax.sharding import PartitionSpec as P

MESH = pl.DeviceIdType.MESH
F32 = jnp.float32
BF16 = jnp.bfloat16
LANES = 128
STAGES = 4
RING = 4


def iota(shape, dim):
    return lax.broadcasted_iota(jnp.int32, shape, dim)


def dot(a, b):
    return jnp.dot(a, b, preferred_element_type=F32)


def await_bytes(ref, sem):
    pltpu.make_async_copy(ref, ref, sem).wait()


def kernel(
    sizes,
    qkv_ref,
    cot_ref,
    dest_ref,
    marks_ref,
    filt_ref,
    out_ref,
    raw,
    stage,
    got,
    marks_all,
    taps,
    bands,
    pos_all,
    counts,
    masks,
    to_seq,
    to_arrival,
    source,
    outgoing,
    final,
    returned,
    ready,
    relay,
    factors,
    dest_here,
    filt_here,
    load_sem,
    stage_send,
    stage_recv,
    mark_send,
    mark_recv,
    factor_send,
    factor_recv,
    final_send,
    final_recv,
    return_send,
    return_recv,
    ready_send,
    ready_recv,
    relay_send,
    relay_recv,
    forward_send,
):
    pipes, ctxs, tps = sizes
    p, c, t = lax.axis_index("pipe"), lax.axis_index("ctx"), lax.axis_index("tp")
    behind = lax.rem(p + pipes - 1, pipes)
    ahead = lax.rem(p + 1, pipes)
    rows = raw.shape[1]
    half_rows = rows // tps
    blocks = rows // 8
    half_blocks = half_rows // 8
    groups = taps.shape[1]
    stage_groups = groups // 2
    plane = ctxs // RING
    deep, flat = c // plane, c % plane
    sign = 1 - 2 * t
    half_cols = ctxs * LANES
    plane_cols = plane * LANES
    crossing = pl.ds(pl.multiple_of((1 - t) * half_rows, half_rows), half_rows)
    group_size = LANES // stage_groups

    barrier = pltpu.get_barrier_semaphore()
    def greet(*peer):
        pl.semaphore_signal(barrier, inc=1, device_id=peer, device_id_type=MESH)

    for j in range(1, ctxs):
        greet(p, lax.rem(c + j, ctxs), t)
    for j in range(ctxs):
        greet(ahead, lax.rem(c + j, ctxs), t)
    greet(ahead, c, 1 - t)
    for step in range(RING // 2, RING):
        depth = lax.rem(deep + sign * step + RING, RING)
        for y in range(plane):
            greet(ahead, depth * plane + y, 1 - t)
            greet(behind, depth * plane + y, 1 - t)

    loads = []
    first_group = pl.multiple_of(c * stage_groups, stage_groups)
    for i, (source_ref, target_ref) in enumerate(
        (
            (cot_ref.at[0], raw.at[0]),
            (qkv_ref.at[0, 0], raw.at[1]),
            (qkv_ref.at[0, 1], raw.at[2]),
            (qkv_ref.at[0, 2], raw.at[3]),
            (dest_ref, dest_here),
            (filt_ref.at[0, pl.ds(first_group, stage_groups)], filt_here.at[0]),
            (filt_ref.at[0, pl.ds(ctxs * stage_groups + first_group, stage_groups)], filt_here.at[1]),
            (marks_ref, marks_all.at[pl.ds(c, 1)]),
        )
    ):
        load = pltpu.make_async_copy(source_ref, target_ref, load_sem.at[i])
        load.start()
        loads.append(load)

    def products(s):
        first, second, half = 2 * (s // 2), 2 * (s // 2) + 1, s % 2

        def one(j, carry):
            col = pl.multiple_of(half * half_cols + j * LANES, LANES)
            a = raw[first, :, pl.ds(col, LANES)].astype(F32)
            b = raw[second, :, pl.ds(col, LANES)].astype(F32)
            stage[s, j] = (a * b).reshape(rows // 8, 8, LANES).astype(BF16)
            return carry

        lax.fori_loop(0, ctxs, one, 0)

    def owner_depth(side_sign, step):
        return lax.rem(deep - side_sign * step + RING, RING)

    def half_span(side):
        return pl.ds(side * half_blocks, half_blocks)

    def send_stage(s):
        if s < 2:
            for step in range(RING // 2, RING):
                span = pl.ds(owner_depth(sign, step) * plane, plane)
                pltpu.make_async_remote_copy(
                    src_ref=stage.at[s, span, half_span(1 - t)],
                    dst_ref=relay.at[s, step - RING // 2],
                    send_sem=relay_send,
                    recv_sem=relay_recv.at[s],
                    device_id=(behind, c, 1 - t),
                    device_id_type=MESH,
                ).start()
        for step in (2, 3, 1, 0):
            for k in range(plane):
                target = owner_depth(sign, step) * plane + lax.rem(flat + k, plane)
                piece, place = stage.at[s, target], got.at[s, c]
                if step >= RING // 2:
                    piece, place = piece.at[half_span(t)], place.at[half_span(t)]
                if step > 0 or k > 0:
                    pltpu.make_async_remote_copy(
                        src_ref=piece,
                        dst_ref=place,
                        send_sem=stage_send.at[s],
                        recv_sem=stage_recv.at[s],
                        device_id=(p, target, t),
                        device_id_type=MESH,
                    ).start()
        got[s, c] = stage[s, c]

    def forward(s):
        for step in range(RING // 2, RING):
            depth = owner_depth(-sign, step)
            if s >= 2:

                def one(y, carry):
                    near = pl.ds(
                        pl.multiple_of(s % 2 * half_cols + depth * plane_cols + y * LANES, LANES),
                        LANES,
                    )
                    key = factors[1 - t, 1, :, near].astype(F32)
                    value = factors[1 - t, 2, :, near].astype(F32)
                    mixed = (key * value).reshape(half_blocks, 8, LANES)
                    relay[s, step - RING // 2, y] = mixed.astype(BF16)
                    return carry

                lax.fori_loop(0, plane, one, 0)
            for k in range(plane):
                y = lax.rem(flat + k, plane)
                pltpu.make_async_remote_copy(
                    src_ref=relay.at[s, step - RING // 2, y],
                    dst_ref=got.at[s, c, half_span(t)],
                    send_sem=forward_send,
                    recv_sem=stage_recv.at[s],
                    device_id=(ahead, depth * plane + y, 1 - t),
                    device_id_type=MESH,
                ).start()

    arrays = (cot_ref.at[0], qkv_ref.at[0, 1], qkv_ref.at[0, 2])

    def near_factors():
        span = pl.ds(pl.multiple_of(t * half_rows, half_rows), half_rows)
        return [
            pltpu.make_async_remote_copy(
                src_ref=ref.at[span],
                dst_ref=factors.at[t, i],
                send_sem=factor_send.at[2],
                recv_sem=factor_recv.at[2],
                device_id=(behind, c, t),
                device_id_type=MESH,
            )
            for i, ref in enumerate(arrays)
        ]

    def far_factors(part):
        copies = []
        for half in range(2):
            for step in range(RING // 2, RING):
                col = half * half_cols + owner_depth(sign, step) * plane_cols
                span = pl.ds(pl.multiple_of(col, plane_cols), plane_cols)
                for i in part:
                    copies.append(
                        pltpu.make_async_remote_copy(
                            src_ref=arrays[i].at[crossing, span],
                            dst_ref=factors.at[t, i, :, span],
                            send_sem=factor_send.at[min(i, 1)],
                            recv_sem=factor_recv.at[min(i, 1)],
                            device_id=(behind, c, 1 - t),
                            device_id_type=MESH,
                        )
                    )
        return copies

    pl.semaphore_wait(barrier, 3 * ctxs)
    for copy in far_factors((1, 2)):
        copy.start()
    loads[0].wait()
    loads[1].wait()
    products(0)
    for j in range(1, ctxs):
        pltpu.make_async_remote_copy(
            src_ref=marks_ref,
            dst_ref=marks_all.at[pl.ds(c, 1)],
            send_sem=mark_send,
            recv_sem=mark_recv,
            device_id=(p, lax.rem(c + j, ctxs), t),
            device_id_type=MESH,
        ).start()
    send_stage(0)
    products(1)
    send_stage(1)
    loads[2].wait()
    loads[3].wait()
    products(2)
    send_stage(2)
    products(3)
    send_stage(3)
    for copy in far_factors((0,)):
        copy.start()

    for load in loads[4:]:
        load.wait()
    mine = filt_here[...].astype(F32).reshape(groups, LANES).astype(BF16)
    lag, lane = iota((LANES, 2 * LANES), 0), iota((LANES, 2 * LANES), 1)
    taps[0] = dot(mine, (lane == LANES - lag).astype(BF16))
    taps[1] = dot(mine, (lane == lag).astype(BF16))

    def one_band(i, carry):
        for way in range(2):
            row = jnp.broadcast_to(taps[way, pl.ds(i, 1), :], (LANES, 2 * LANES))
            band = pltpu.roll(row, 0, 1, stride=1, stride_axis=0)
            bands[way, i] = band.astype(BF16)
        return carry

    lax.fori_loop(0, groups, one_band, 0)

    for s in range(2):
        await_bytes(relay.at[s], relay_recv.at[s])
        forward(s)

    slots = ctxs * ctxs
    dest = jnp.broadcast_to(dest_here[pl.ds(p, 1), :], (ctxs, slots))
    entry, tile = iota((ctxs, slots), 1), iota((ctxs, slots), 0)
    slot = jnp.where(entry % ctxs == tile, dest - tile * ctxs, 0).astype(F32).astype(BF16)
    spread = (iota((slots, LANES), 0) // ctxs == iota((slots, LANES), 1) // 8).astype(BF16)
    pos_all[...] = dot(slot, spread) * 8.0 + (iota((ctxs, LANES), 1) % 8).astype(F32)

    await_bytes(marks_all.at[pl.ds(0, ctxs - 1)], mark_recv)
    down = iota((LANES, LANES), 0)
    across = iota((LANES, LANES), 1)
    owner = iota((ctxs, LANES), 0) == iota((ctxs, LANES), 1) // 8

    def one_order(b, table):
        pick = (down == b * 8 + across % 8).astype(BF16)
        marks = dot(marks_all[...].astype(F32).astype(BF16), pick)
        marks = jnp.sum(jnp.where(owner, marks, 0.0), axis=0, keepdims=True)
        pos = pos_all[pl.ds(b, 1), :]
        rank = down.astype(F32)
        place = (pos == rank).astype(F32)
        to_seq[b] = place.astype(BF16)
        to_arrival[b] = place.T.astype(BF16)
        count = jnp.sum(jnp.where(pos <= rank, marks, 0.0), axis=1, keepdims=True)
        return jnp.where(across == b, count, table)

    table = lax.fori_loop(0, ctxs, one_order, jnp.zeros((LANES, LANES), F32))
    counts[...] = table.T

    def one_mask(b, carry):
        here = counts[pl.ds(b, 1), :]
        total = here[:, LANES - 1 :]
        prior = counts[pl.ds(jnp.maximum(b - 1, 0), 1), :]
        prior = jnp.where(b > 0, prior - prior[:, LANES - 1 :], -1.0)
        later = counts[pl.ds(jnp.minimum(b + 1, ctxs - 1), 1), :]
        later = jnp.where(b < ctxs - 1, later + total, -1.0)
        column = jnp.broadcast_to(here, (LANES, LANES)).T
        column = jnp.concatenate([column, column], axis=1)
        masks[0, b] = (column == jnp.concatenate([prior, here], axis=1)).astype(F32).astype(BF16)
        masks[1, b] = (column == jnp.concatenate([here, later], axis=1)).astype(F32).astype(BF16)
        return carry

    lax.fori_loop(0, ctxs, one_mask, 0)
    source[pl.ds(0, LANES), :] = jnp.zeros((LANES, LANES), BF16)
    source[pl.ds((ctxs + 1) * LANES, LANES), :] = jnp.zeros((LANES, LANES), BF16)
    group_of_lane = iota((LANES, LANES), 1) // group_size

    def convolve(s):
        way, half = 1 - s // 2, s % 2

        def order(b, carry):
            block = got[s, :, b].astype(F32).reshape(LANES, LANES).astype(BF16)
            at = pl.multiple_of((b + 1) * LANES, LANES)
            source[pl.ds(at, LANES), :] = dot(to_seq[b], block).astype(BF16)
            return carry

        lax.fori_loop(0, ctxs, order, 0, unroll=8)

        def one_tile(b, carry):
            window = source[pl.ds(pl.multiple_of((b + way) * LANES, LANES), 2 * LANES), :]
            mask = masks[way, b]
            total = jnp.zeros((LANES, LANES), F32)
            for g in range(stage_groups):
                band = bands[way, half * stage_groups + g] * mask
                total = jnp.where(group_of_lane == g, dot(band, window), total)
            back = dot(to_arrival[b], total.astype(BF16))
            outgoing[s, :, b] = back.reshape(ctxs, 8, LANES).astype(BF16)
            return carry

        lax.fori_loop(0, ctxs, one_tile, 0, unroll=4)

    def send_final(s):
        for step in range(RING // 2):
            for k in range(plane):
                y = lax.rem(flat + k, plane)
                target = lax.rem(deep + sign * step + RING, RING) * plane + y
                piece = outgoing.at[s, target, pl.ds((1 - t) * half_blocks, half_blocks)]
                if step == 0 and k == 0:
                    returned[s, step * plane + flat] = outgoing[s, c, pl.ds((1 - t) * half_blocks, half_blocks)]
                else:
                    pltpu.make_async_remote_copy(
                        src_ref=piece,
                        dst_ref=returned.at[s, step * plane + flat],
                        send_sem=return_send.at[s],
                        recv_sem=return_recv.at[s],
                        device_id=(p, target, t),
                        device_id_type=MESH,
                    ).start()
        for step in (2, 3, 1, 0):
            for k in range(plane):
                y = lax.rem(flat + k, plane)
                target = lax.rem(deep + sign * step + RING, RING) * plane + y
                for side in (t, 1 - t) if step >= RING // 2 else (t,):
                    pltpu.make_async_remote_copy(
                        src_ref=outgoing.at[s, target, pl.ds(side * half_blocks, half_blocks)],
                        dst_ref=final.at[s, t * ctxs + c],
                        send_sem=final_send.at[s],
                        recv_sem=final_recv.at[s],
                        device_id=(behind, target, side),
                        device_id_type=MESH,
                    ).start()

    def outputs(s):
        return ((0, 0, 0),) if s >= 2 else ((1, 2, 3), (2, 1, 2))

    def ready_copies(s):
        half = s % 2
        copies = []
        for step in range(RING // 2):
            col = half * half_cols + owner_depth(sign, step) * plane_cols
            span = pl.ds(pl.multiple_of(t * 2 * half_cols + col, plane_cols), plane_cols)
            for out, _, _ in outputs(s):
                copies.append(
                    pltpu.make_async_remote_copy(
                        src_ref=ready.at[half, step, out],
                        dst_ref=out_ref.at[0, out, :, span],
                        send_sem=ready_send,
                        recv_sem=ready_recv,
                        device_id=(behind, c, 1 - t),
                        device_id_type=MESH,
                    )
                )
        return copies

    def pass_on(s):
        half = s % 2
        await_bytes(returned.at[s, pl.ds(0, ctxs // 2 - 1)], return_recv.at[s])
        for step in range(RING // 2):

            def one(y, carry):
                col = half * half_cols + owner_depth(sign, step) * plane_cols + y * LANES
                near = pl.ds(pl.multiple_of(col, LANES), LANES)
                at = pl.ds(pl.multiple_of(y * LANES, LANES), LANES)
                conv = returned[s, step * plane + y].astype(F32).reshape(half_rows, LANES)
                for out, _, factor in outputs(s):
                    value = raw[factor, crossing, near].astype(F32)
                    ready[half, step, out, :, at] = (value * conv).astype(BF16)
                return carry

            lax.fori_loop(0, plane, one, 0, unroll=True)
        for copy in ready_copies(s):
            copy.start()

    await_bytes(factors.at[0, pl.ds(0, 2), :, pl.ds(0, half_cols)], factor_recv.at[1])
    forward(2)
    forward(3)
    for s in range(STAGES):
        await_bytes(got.at[s, pl.ds(0, ctxs - 1)], stage_recv.at[s])
        convolve(s)
        send_final(s)
        if s >= 1:
            pass_on(s - 1)
        if s == 0:
            for copy in near_factors():
                copy.start()
    pass_on(STAGES - 1)

    await_bytes(factors.at[0], factor_recv.at[2])
    await_bytes(factors.at[0, 0, :, pl.ds(0, half_cols)], factor_recv.at[0])

    def finish(s):
        half = s % 2

        def one(side, depth, y):
            col = half * half_cols + depth * plane_cols + y * LANES
            near = pl.ds(pl.multiple_of(col, LANES), LANES)
            far = pl.ds(pl.multiple_of(side * 2 * half_cols + col, LANES), LANES)
            conv = final[s, side * ctxs + depth * plane + y].astype(F32).reshape(half_rows, LANES)
            for out, factor, _ in outputs(s):
                value = factors[side, factor, :, near].astype(F32)
                out_ref[0, out, :, far] = (value * conv).astype(BF16)

        def own(i, carry):
            one(t, i // plane, i % plane)
            return carry

        lax.fori_loop(0, ctxs, own, 0, unroll=4)

        def other(i, carry):
            one(1 - t, owner_depth(-sign, RING // 2 + i // plane), i % plane)
            return carry

        lax.fori_loop(0, ctxs // 2, other, 0, unroll=4)

    for s in range(STAGES):
        await_bytes(final.at[s, pl.ds(0, ctxs + ctxs // 2)], final_recv.at[s])
        finish(s)
    await_bytes(out_ref.at[0, :, :, pl.ds(0, half_cols)], ready_recv)

    await_bytes(marks_all.at[pl.ds(0, ctxs - 1)], mark_send)
    for s in range(STAGES):
        await_bytes(stage.at[s, pl.ds(0, 3 * ctxs // 4 - 1)], stage_send.at[s])
        await_bytes(returned.at[s, pl.ds(0, ctxs // 2 - 1)], return_send.at[s])
        await_bytes(final.at[s, pl.ds(0, ctxs + ctxs // 2)], final_send.at[s])
    await_bytes(factors.at[0], factor_send.at[2])
    await_bytes(factors.at[0, pl.ds(0, 2), :, pl.ds(0, half_cols)], factor_send.at[1])
    await_bytes(relay.at[pl.ds(0, 2)], relay_send)
    await_bytes(relay, forward_send)
    await_bytes(factors.at[0, 0, :, pl.ds(0, half_cols)], factor_send.at[0])
    await_bytes(out_ref.at[0, :, :, pl.ds(0, half_cols)], ready_send)


def shards(sizes, qkv_proj, cotangent, block_dest, doc_start, mr_filter):
    pipes, ctxs, tps = sizes
    rows, channels = cotangent.shape[1:]
    taps = mr_filter.shape[2]
    groups = mr_filter.shape[1] // ctxs
    half_rows = rows // tps
    blocks = rows // 8
    dma = pltpu.SemaphoreType.DMA
    return pl.pallas_call(
        functools.partial(kernel, sizes),
        out_shape=jax.ShapeDtypeStruct((1, 3, half_rows, channels * tps), BF16),
        in_specs=[pl.BlockSpec(memory_space=pltpu.HBM)] * 5,
        out_specs=pl.BlockSpec(memory_space=pltpu.VMEM),
        scratch_shapes=[
            pltpu.VMEM((4, rows, channels), BF16),
            pltpu.VMEM((STAGES, ctxs, blocks, 8, LANES), BF16),
            pltpu.VMEM((STAGES, ctxs, blocks, 8, LANES), BF16),
            pltpu.VMEM((ctxs, LANES), jnp.int32),
            pltpu.VMEM((2, groups, 2 * taps), F32),
            pltpu.VMEM((2, groups, taps, 2 * taps), BF16),
            pltpu.VMEM((ctxs, LANES), F32),
            pltpu.VMEM((LANES, LANES), F32),
            pltpu.VMEM((2, ctxs, LANES, 2 * LANES), BF16),
            pltpu.VMEM((ctxs, LANES, LANES), BF16),
            pltpu.VMEM((ctxs, LANES, LANES), BF16),
            pltpu.VMEM(((ctxs + 2) * LANES, LANES), BF16),
            pltpu.VMEM((STAGES, ctxs, blocks, 8, LANES), BF16),
            pltpu.VMEM((STAGES, tps * ctxs, blocks // tps, 8, LANES), BF16),
            pltpu.VMEM((STAGES, ctxs // 2, blocks // tps, 8, LANES), BF16),
            pltpu.VMEM((2, RING // 2, 3, half_rows, ctxs // RING * LANES), BF16),
            pltpu.VMEM((STAGES, RING // 2, ctxs // RING, blocks // tps, 8, LANES), BF16),
            pltpu.VMEM((tps, 3, half_rows, channels), BF16),
            pltpu.VMEM(block_dest.shape, jnp.int32),
            pltpu.VMEM((2, groups // 2, taps), BF16),
            dma((8,)),
            dma((STAGES,)),
            dma((STAGES,)),
            dma,
            dma,
            dma((3,)),
            dma((3,)),
            dma((STAGES,)),
            dma((STAGES,)),
            dma((STAGES,)),
            dma((STAGES,)),
            dma,
            dma,
            dma,
            dma((2,)),
            dma,
        ],
        compiler_params=pltpu.CompilerParams(
            collective_id=0, has_side_effects=True, vmem_limit_bytes=44 << 20
        ),
        name="hyena_input_grads",
    )(*(pltpu.with_memory_space_constraint(x, pltpu.HBM) for x in (qkv_proj, cotangent, block_dest, doc_start, mr_filter)))


def solution(mesh):
    sizes = (mesh.shape["pipe"], mesh.shape["ctx"], mesh.shape["tp"])
    placed = (
        P("pipe", None, "ctx", "tp"),
        P("pipe", "ctx", "tp"),
        P(),
        P("pipe", "ctx"),
        P("pipe", "tp", None),
    )
    return jax.shard_map(
        functools.partial(shards, sizes),
        mesh=mesh,
        in_specs=placed,
        out_specs=P("pipe", None, ("ctx", "tp"), None),
        check_vma=False,
    )
```

```python
import functools

import jax
import jax.numpy as jnp
from jax import lax
from jax.experimental import pallas as pl
from jax.experimental.pallas import tpu as pltpu
from jax.sharding import PartitionSpec as P

MESH = pl.DeviceIdType.MESH
F32 = jnp.float32
BF16 = jnp.bfloat16
LANES = 128
STAGES = 4
RING = 4


def iota(shape, dim):
    return lax.broadcasted_iota(jnp.int32, shape, dim)


def dot(a, b):
    return jnp.dot(a, b, preferred_element_type=F32)


def await_bytes(ref, sem):
    pltpu.make_async_copy(ref, ref, sem).wait()


def kernel(
    sizes,
    qkv_ref,
    cot_ref,
    dest_ref,
    marks_ref,
    filt_ref,
    out_ref,
    raw,
    stage,
    got,
    marks_all,
    taps,
    bands,
    pos_all,
    counts,
    masks,
    to_seq,
    to_arrival,
    source,
    outgoing,
    final,
    returned,
    ready,
    relay,
    factors,
    dest_here,
    filt_here,
    load_sem,
    stage_send,
    stage_recv,
    mark_send,
    mark_recv,
    factor_send,
    factor_recv,
    final_send,
    final_recv,
    return_send,
    return_recv,
    ready_send,
    ready_recv,
    relay_send,
    relay_recv,
    forward_send,
):
    pipes, ctxs, tps = sizes
    p, c, t = lax.axis_index("pipe"), lax.axis_index("ctx"), lax.axis_index("tp")
    behind = lax.rem(p + pipes - 1, pipes)
    ahead = lax.rem(p + 1, pipes)
    rows = raw.shape[1]
    half_rows = rows // tps
    blocks = rows // 8
    half_blocks = half_rows // 8
    groups = taps.shape[1]
    stage_groups = groups // 2
    plane = ctxs // RING
    deep, flat = c // plane, c % plane
    sign = 1 - 2 * t
    half_cols = ctxs * LANES
    plane_cols = plane * LANES
    crossing = pl.ds(pl.multiple_of((1 - t) * half_rows, half_rows), half_rows)
    group_size = LANES // stage_groups

    barrier = pltpu.get_barrier_semaphore()
    def greet(*peer):
        pl.semaphore_signal(barrier, inc=1, device_id=peer, device_id_type=MESH)

    for j in range(1, ctxs):
        greet(p, lax.rem(c + j, ctxs), t)
    for j in range(ctxs):
        greet(ahead, lax.rem(c + j, ctxs), t)
    greet(ahead, c, 1 - t)
    for step in range(RING // 2, RING):
        depth = lax.rem(deep + sign * step + RING, RING)
        for y in range(plane):
            greet(ahead, depth * plane + y, 1 - t)
            greet(behind, depth * plane + y, 1 - t)

    loads = []
    first_group = pl.multiple_of(c * stage_groups, stage_groups)
    for i, (source_ref, target_ref) in enumerate(
        (
            (cot_ref.at[0], raw.at[0]),
            (qkv_ref.at[0, 0], raw.at[1]),
            (qkv_ref.at[0, 1], raw.at[2]),
            (qkv_ref.at[0, 2], raw.at[3]),
            (dest_ref, dest_here),
            (filt_ref.at[0, pl.ds(first_group, stage_groups)], filt_here.at[0]),
            (filt_ref.at[0, pl.ds(ctxs * stage_groups + first_group, stage_groups)], filt_here.at[1]),
            (marks_ref, marks_all.at[pl.ds(c, 1)]),
        )
    ):
        load = pltpu.make_async_copy(source_ref, target_ref, load_sem.at[i])
        load.start()
        loads.append(load)

    def products(s):
        first, second, half = 2 * (s // 2), 2 * (s // 2) + 1, s % 2

        def one(j, carry):
            col = pl.multiple_of(half * half_cols + j * LANES, LANES)
            a = raw[first, :, pl.ds(col, LANES)].astype(F32)
            b = raw[second, :, pl.ds(col, LANES)].astype(F32)
            stage[s, j] = (a * b).reshape(rows // 8, 8, LANES).astype(BF16)
            return carry

        lax.fori_loop(0, ctxs, one, 0)

    def owner_depth(side_sign, step):
        return lax.rem(deep - side_sign * step + RING, RING)

    def half_span(side):
        return pl.ds(side * half_blocks, half_blocks)

    def send_stage(s):
        if s < 2:
            for step in range(RING // 2, RING):
                span = pl.ds(owner_depth(sign, step) * plane, plane)
                pltpu.make_async_remote_copy(
                    src_ref=stage.at[s, span, half_span(1 - t)],
                    dst_ref=relay.at[s, step - RING // 2],
                    send_sem=relay_send,
                    recv_sem=relay_recv.at[s],
                    device_id=(behind, c, 1 - t),
                    device_id_type=MESH,
                ).start()
        for step in (2, 3, 1, 0):
            for k in range(plane):
                target = owner_depth(sign, step) * plane + lax.rem(flat + k, plane)
                piece, place = stage.at[s, target], got.at[s, c]
                if step >= RING // 2:
                    piece, place = piece.at[half_span(t)], place.at[half_span(t)]
                if step > 0 or k > 0:
                    pltpu.make_async_remote_copy(
                        src_ref=piece,
                        dst_ref=place,
                        send_sem=stage_send.at[s],
                        recv_sem=stage_recv.at[s],
                        device_id=(p, target, t),
                        device_id_type=MESH,
                    ).start()
        got[s, c] = stage[s, c]

    def forward(s):
        for step in range(RING // 2, RING):
            depth = owner_depth(-sign, step)
            if s >= 2:

                def one(y, carry):
                    near = pl.ds(
                        pl.multiple_of(s % 2 * half_cols + depth * plane_cols + y * LANES, LANES),
                        LANES,
                    )
                    key = factors[1 - t, 1, :, near].astype(F32)
                    value = factors[1 - t, 2, :, near].astype(F32)
                    mixed = (key * value).reshape(half_blocks, 8, LANES)
                    relay[s, step - RING // 2, y] = mixed.astype(BF16)
                    return carry

                lax.fori_loop(0, plane, one, 0)
            for k in range(plane):
                y = lax.rem(flat + k, plane)
                pltpu.make_async_remote_copy(
                    src_ref=relay.at[s, step - RING // 2, y],
                    dst_ref=got.at[s, c, half_span(t)],
                    send_sem=forward_send,
                    recv_sem=stage_recv.at[s],
                    device_id=(ahead, depth * plane + y, 1 - t),
                    device_id_type=MESH,
                ).start()

    arrays = (cot_ref.at[0], qkv_ref.at[0, 1], qkv_ref.at[0, 2])

    def near_factors():
        span = pl.ds(pl.multiple_of(t * half_rows, half_rows), half_rows)
        return [
            pltpu.make_async_remote_copy(
                src_ref=ref.at[span],
                dst_ref=factors.at[t, i],
                send_sem=factor_send.at[2],
                recv_sem=factor_recv.at[2],
                device_id=(behind, c, t),
                device_id_type=MESH,
            )
            for i, ref in enumerate(arrays)
        ]

    def far_factors(part):
        copies = []
        for half in range(2):
            for step in range(RING // 2, RING):
                col = half * half_cols + owner_depth(sign, step) * plane_cols
                span = pl.ds(pl.multiple_of(col, plane_cols), plane_cols)
                for i in part:
                    copies.append(
                        pltpu.make_async_remote_copy(
                            src_ref=arrays[i].at[crossing, span],
                            dst_ref=factors.at[t, i, :, span],
                            send_sem=factor_send.at[min(i, 1)],
                            recv_sem=factor_recv.at[min(i, 1)],
                            device_id=(behind, c, 1 - t),
                            device_id_type=MESH,
                        )
                    )
        return copies

    loads[0].wait()
    loads[1].wait()
    products(0)
    pl.semaphore_wait(barrier, 3 * ctxs)
    for copy in far_factors((1, 2)):
        copy.start()
    for j in range(1, ctxs):
        pltpu.make_async_remote_copy(
            src_ref=marks_ref,
            dst_ref=marks_all.at[pl.ds(c, 1)],
            send_sem=mark_send,
            recv_sem=mark_recv,
            device_id=(p, lax.rem(c + j, ctxs), t),
            device_id_type=MESH,
        ).start()
    send_stage(0)
    products(1)
    send_stage(1)
    for copy in far_factors((0,)):
        copy.start()
    loads[2].wait()
    loads[3].wait()
    products(2)
    send_stage(2)
    products(3)
    send_stage(3)

    for load in loads[4:]:
        load.wait()
    mine = filt_here[...].astype(F32).reshape(groups, LANES).astype(BF16)
    lag, lane = iota((LANES, 2 * LANES), 0), iota((LANES, 2 * LANES), 1)
    taps[0] = dot(mine, (lane == LANES - lag).astype(BF16))
    taps[1] = dot(mine, (lane == lag).astype(BF16))

    def one_band(i, carry):
        for way in range(2):
            row = jnp.broadcast_to(taps[way, pl.ds(i, 1), :], (LANES, 2 * LANES))
            band = pltpu.roll(row, 0, 1, stride=1, stride_axis=0)
            bands[way, i] = band.astype(BF16)
        return carry

    lax.fori_loop(0, groups, one_band, 0)

    for s in range(2):
        await_bytes(relay.at[s], relay_recv.at[s])
        forward(s)

    slots = ctxs * ctxs
    dest = jnp.broadcast_to(dest_here[pl.ds(p, 1), :], (ctxs, slots))
    entry, tile = iota((ctxs, slots), 1), iota((ctxs, slots), 0)
    slot = jnp.where(entry % ctxs == tile, dest - tile * ctxs, 0).astype(F32).astype(BF16)
    spread = (iota((slots, LANES), 0) // ctxs == iota((slots, LANES), 1) // 8).astype(BF16)
    pos_all[...] = dot(slot, spread) * 8.0 + (iota((ctxs, LANES), 1) % 8).astype(F32)

    await_bytes(marks_all.at[pl.ds(0, ctxs - 1)], mark_recv)
    down = iota((LANES, LANES), 0)
    across = iota((LANES, LANES), 1)
    owner = iota((ctxs, LANES), 0) == iota((ctxs, LANES), 1) // 8

    def one_order(b, table):
        pick = (down == b * 8 + across % 8).astype(BF16)
        marks = dot(marks_all[...].astype(F32).astype(BF16), pick)
        marks = jnp.sum(jnp.where(owner, marks, 0.0), axis=0, keepdims=True)
        pos = pos_all[pl.ds(b, 1), :]
        rank = down.astype(F32)
        place = (pos == rank).astype(F32)
        to_seq[b] = place.astype(BF16)
        to_arrival[b] = place.T.astype(BF16)
        count = jnp.sum(jnp.where(pos <= rank, marks, 0.0), axis=1, keepdims=True)
        return jnp.where(across == b, count, table)

    table = lax.fori_loop(0, ctxs, one_order, jnp.zeros((LANES, LANES), F32))
    counts[...] = table.T

    def one_mask(b, carry):
        here = counts[pl.ds(b, 1), :]
        total = here[:, LANES - 1 :]
        prior = counts[pl.ds(jnp.maximum(b - 1, 0), 1), :]
        prior = jnp.where(b > 0, prior - prior[:, LANES - 1 :], -1.0)
        later = counts[pl.ds(jnp.minimum(b + 1, ctxs - 1), 1), :]
        later = jnp.where(b < ctxs - 1, later + total, -1.0)
        column = jnp.broadcast_to(here, (LANES, LANES)).T
        column = jnp.concatenate([column, column], axis=1)
        masks[0, b] = (column == jnp.concatenate([prior, here], axis=1)).astype(F32).astype(BF16)
        masks[1, b] = (column == jnp.concatenate([here, later], axis=1)).astype(F32).astype(BF16)
        return carry

    lax.fori_loop(0, ctxs, one_mask, 0)
    source[pl.ds(0, LANES), :] = jnp.zeros((LANES, LANES), BF16)
    source[pl.ds((ctxs + 1) * LANES, LANES), :] = jnp.zeros((LANES, LANES), BF16)
    group_of_lane = iota((LANES, LANES), 1) // group_size

    def convolve(s):
        way, half = 1 - s // 2, s % 2

        def order(b, carry):
            block = got[s, :, b].astype(F32).reshape(LANES, LANES).astype(BF16)
            at = pl.multiple_of((b + 1) * LANES, LANES)
            source[pl.ds(at, LANES), :] = dot(to_seq[b], block).astype(BF16)
            return carry

        lax.fori_loop(0, ctxs, order, 0, unroll=8)

        def one_tile(b, carry):
            window = source[pl.ds(pl.multiple_of((b + way) * LANES, LANES), 2 * LANES), :]
            mask = masks[way, b]
            total = jnp.zeros((LANES, LANES), F32)
            for g in range(stage_groups):
                band = bands[way, half * stage_groups + g] * mask
                total = jnp.where(group_of_lane == g, dot(band, window), total)
            back = dot(to_arrival[b], total.astype(BF16))
            outgoing[s, :, b] = back.reshape(ctxs, 8, LANES).astype(BF16)
            return carry

        lax.fori_loop(0, ctxs, one_tile, 0, unroll=4)

    def send_final(s):
        for step in range(RING // 2):
            for k in range(plane):
                y = lax.rem(flat + k, plane)
                target = lax.rem(deep + sign * step + RING, RING) * plane + y
                piece = outgoing.at[s, target, pl.ds((1 - t) * half_blocks, half_blocks)]
                if step == 0 and k == 0:
                    returned[s, step * plane + flat] = outgoing[s, c, pl.ds((1 - t) * half_blocks, half_blocks)]
                else:
                    pltpu.make_async_remote_copy(
                        src_ref=piece,
                        dst_ref=returned.at[s, step * plane + flat],
                        send_sem=return_send.at[s],
                        recv_sem=return_recv.at[s],
                        device_id=(p, target, t),
                        device_id_type=MESH,
                    ).start()
        for step in (2, 3, 1, 0):
            for k in range(plane):
                y = lax.rem(flat + k, plane)
                target = lax.rem(deep + sign * step + RING, RING) * plane + y
                for side in (t, 1 - t) if step >= RING // 2 else (t,):
                    pltpu.make_async_remote_copy(
                        src_ref=outgoing.at[s, target, pl.ds(side * half_blocks, half_blocks)],
                        dst_ref=final.at[s, t * ctxs + c],
                        send_sem=final_send.at[s],
                        recv_sem=final_recv.at[s],
                        device_id=(behind, target, side),
                        device_id_type=MESH,
                    ).start()

    def outputs(s):
        return ((0, 0, 0),) if s >= 2 else ((1, 2, 3), (2, 1, 2))

    def ready_copies(s):
        half = s % 2
        copies = []
        for step in range(RING // 2):
            col = half * half_cols + owner_depth(sign, step) * plane_cols
            span = pl.ds(pl.multiple_of(t * 2 * half_cols + col, plane_cols), plane_cols)
            for out, _, _ in outputs(s):
                copies.append(
                    pltpu.make_async_remote_copy(
                        src_ref=ready.at[half, step, out],
                        dst_ref=out_ref.at[0, out, :, span],
                        send_sem=ready_send,
                        recv_sem=ready_recv,
                        device_id=(behind, c, 1 - t),
                        device_id_type=MESH,
                    )
                )
        return copies

    def pass_on(s):
        half = s % 2
        await_bytes(returned.at[s, pl.ds(0, ctxs // 2 - 1)], return_recv.at[s])
        for step in range(RING // 2):

            def one(y, carry):
                col = half * half_cols + owner_depth(sign, step) * plane_cols + y * LANES
                near = pl.ds(pl.multiple_of(col, LANES), LANES)
                at = pl.ds(pl.multiple_of(y * LANES, LANES), LANES)
                conv = returned[s, step * plane + y].astype(F32).reshape(half_rows, LANES)
                for out, _, factor in outputs(s):
                    value = raw[factor, crossing, near].astype(F32)
                    ready[half, step, out, :, at] = (value * conv).astype(BF16)
                return carry

            lax.fori_loop(0, plane, one, 0, unroll=True)
        for copy in ready_copies(s):
            copy.start()

    await_bytes(factors.at[0, pl.ds(0, 2), :, pl.ds(0, half_cols)], factor_recv.at[1])
    forward(2)
    forward(3)
    for s in range(STAGES):
        await_bytes(got.at[s, pl.ds(0, ctxs - 1)], stage_recv.at[s])
        convolve(s)
        send_final(s)
        if s >= 1:
            pass_on(s - 1)
        if s == 0:
            for copy in near_factors():
                copy.start()
    pass_on(STAGES - 1)

    await_bytes(factors.at[0], factor_recv.at[2])
    await_bytes(factors.at[0, 0, :, pl.ds(0, half_cols)], factor_recv.at[0])

    def finish(s):
        half = s % 2

        def one(side, depth, y):
            col = half * half_cols + depth * plane_cols + y * LANES
            near = pl.ds(pl.multiple_of(col, LANES), LANES)
            far = pl.ds(pl.multiple_of(side * 2 * half_cols + col, LANES), LANES)
            conv = final[s, side * ctxs + depth * plane + y].astype(F32).reshape(half_rows, LANES)
            for out, factor, _ in outputs(s):
                value = factors[side, factor, :, near].astype(F32)
                out_ref[0, out, :, far] = (value * conv).astype(BF16)

        def own(i, carry):
            one(t, i // plane, i % plane)
            return carry

        lax.fori_loop(0, ctxs, own, 0, unroll=4)

        def other(i, carry):
            one(1 - t, owner_depth(-sign, RING // 2 + i // plane), i % plane)
            return carry

        lax.fori_loop(0, ctxs // 2, other, 0, unroll=4)

    for s in range(STAGES):
        await_bytes(final.at[s, pl.ds(0, ctxs + ctxs // 2)], final_recv.at[s])
        finish(s)
    await_bytes(out_ref.at[0, :, :, pl.ds(0, half_cols)], ready_recv)

    await_bytes(marks_all.at[pl.ds(0, ctxs - 1)], mark_send)
    for s in range(STAGES):
        await_bytes(stage.at[s, pl.ds(0, 3 * ctxs // 4 - 1)], stage_send.at[s])
        await_bytes(returned.at[s, pl.ds(0, ctxs // 2 - 1)], return_send.at[s])
        await_bytes(final.at[s, pl.ds(0, ctxs + ctxs // 2)], final_send.at[s])
    await_bytes(factors.at[0], factor_send.at[2])
    await_bytes(factors.at[0, pl.ds(0, 2), :, pl.ds(0, half_cols)], factor_send.at[1])
    await_bytes(relay.at[pl.ds(0, 2)], relay_send)
    await_bytes(relay, forward_send)
    await_bytes(factors.at[0, 0, :, pl.ds(0, half_cols)], factor_send.at[0])
    await_bytes(out_ref.at[0, :, :, pl.ds(0, half_cols)], ready_send)


def shards(sizes, qkv_proj, cotangent, block_dest, doc_start, mr_filter):
    pipes, ctxs, tps = sizes
    rows, channels = cotangent.shape[1:]
    taps = mr_filter.shape[2]
    groups = mr_filter.shape[1] // ctxs
    half_rows = rows // tps
    blocks = rows // 8
    dma = pltpu.SemaphoreType.DMA
    return pl.pallas_call(
        functools.partial(kernel, sizes),
        out_shape=jax.ShapeDtypeStruct((1, 3, half_rows, channels * tps), BF16),
        in_specs=[pl.BlockSpec(memory_space=pltpu.HBM)] * 5,
        out_specs=pl.BlockSpec(memory_space=pltpu.VMEM),
        scratch_shapes=[
            pltpu.VMEM((4, rows, channels), BF16),
            pltpu.VMEM((STAGES, ctxs, blocks, 8, LANES), BF16),
            pltpu.VMEM((STAGES, ctxs, blocks, 8, LANES), BF16),
            pltpu.VMEM((ctxs, LANES), jnp.int32),
            pltpu.VMEM((2, groups, 2 * taps), F32),
            pltpu.VMEM((2, groups, taps, 2 * taps), BF16),
            pltpu.VMEM((ctxs, LANES), F32),
            pltpu.VMEM((LANES, LANES), F32),
            pltpu.VMEM((2, ctxs, LANES, 2 * LANES), BF16),
            pltpu.VMEM((ctxs, LANES, LANES), BF16),
            pltpu.VMEM((ctxs, LANES, LANES), BF16),
            pltpu.VMEM(((ctxs + 2) * LANES, LANES), BF16),
            pltpu.VMEM((STAGES, ctxs, blocks, 8, LANES), BF16),
            pltpu.VMEM((STAGES, tps * ctxs, blocks // tps, 8, LANES), BF16),
            pltpu.VMEM((STAGES, ctxs // 2, blocks // tps, 8, LANES), BF16),
            pltpu.VMEM((2, RING // 2, 3, half_rows, ctxs // RING * LANES), BF16),
            pltpu.VMEM((STAGES, RING // 2, ctxs // RING, blocks // tps, 8, LANES), BF16),
            pltpu.VMEM((tps, 3, half_rows, channels), BF16),
            pltpu.VMEM(block_dest.shape, jnp.int32),
            pltpu.VMEM((2, groups // 2, taps), BF16),
            dma((8,)),
            dma((STAGES,)),
            dma((STAGES,)),
            dma,
            dma,
            dma((3,)),
            dma((3,)),
            dma((STAGES,)),
            dma((STAGES,)),
            dma((STAGES,)),
            dma((STAGES,)),
            dma,
            dma,
            dma,
            dma((2,)),
            dma,
        ],
        compiler_params=pltpu.CompilerParams(
            collective_id=0, has_side_effects=True, vmem_limit_bytes=44 << 20
        ),
        name="hyena_input_grads",
    )(*(pltpu.with_memory_space_constraint(x, pltpu.HBM) for x in (qkv_proj, cotangent, block_dest, doc_start, mr_filter)))


def solution(mesh):
    sizes = (mesh.shape["pipe"], mesh.shape["ctx"], mesh.shape["tp"])
    placed = (
        P("pipe", None, "ctx", "tp"),
        P("pipe", "ctx", "tp"),
        P(),
        P("pipe", "ctx"),
        P("pipe", "tp", None),
    )
    return jax.shard_map(
        functools.partial(shards, sizes),
        mesh=mesh,
        in_specs=placed,
        out_specs=P("pipe", None, ("ctx", "tp"), None),
        check_vma=False,
    )
```
